512 devices in a mesh: chan: 128 (over x, z_lo, y), cross: 4 (over z_hi, core).
Axes of the slice: x: 4, y: 4, z: 16 (z_hi: 2, z_lo: 8; z = z_hi * 8 + z_lo), core: 2. Of those that a mesh axis runs over, the one named last changes fastest.
Arguments:
- positions: float32 [2, 512, 64, 128], P(None, 'chan', 'cross'), may hold values from 0 to 1
- velocity: float32 [2, 512, 64, 128], P(None, 'chan', 'cross'), may hold values from -4 to 4
- density: float32 [512, 64, 128], P('chan', 'cross'), may hold values from 0.8 to 1.2
- counts: int32 [512, 64], P('chan', 'cross'), may hold values from 0 to 128, as said below
Outputs:
- new_fields: float32 [5, 512, 64, 128], P(None, 'chan', 'cross')
- lowest_density: float32 [], replicated
The draws below stay inside these ranges and needn't reach their ends.
Inputs may be any that keep to these rules, and one draw needn't show every extreme that they name: `counts`: in every channel column the bins from cross index 0 up to some height hold particles and those above are empty; the height is 56 or more; the bins at cross index 0 hold 128 particles.
All inputs are finite; a program needn't handle non-finite values.
Results may differ from the reference program's by a relative error of at most 0.0001.
Values sent between devices are 32-bit elements; how exact they have to be, the bound alone decides.
No kernel may reach another device: no remote copies, remote signals or barrier semaphores. Data moves between devices by JAX's collectives and lax.ppermute only.
A program may use at most 64 MiB of HBM per device.

```python
import math
import jax
import jax.numpy as jnp
from jax import lax

S = 128
BY = 16
NBX = 512
NBY = 64


def draw_density(key, part):
    key_phase, key_jitter = jax.random.split(jax.random.fold_in(key, 11))
    along_axis = jnp.arange(NBX, dtype=jnp.float32) / NBX
    across = jnp.arange(NBY, dtype=jnp.float32) / NBY
    wave_phase = jax.random.uniform(key_phase, (), jnp.float32, 0.0, 2.0 * math.pi)
    amplitude = 0.08
    jitter = jax.random.uniform(key_jitter, (NBX, NBY, S), jnp.float32, -0.03, 0.03)
    wave_term = amplitude * jnp.sin(2.0 * math.pi * along_axis + wave_phase)
    return 1.0 + wave_term[:, None, None] + 0.04 * (1.0 - across)[None, :, None] + jitter


def draw_counts(key, part):
    key_height, key_fill = jax.random.split(jax.random.fold_in(key, 23))
    height = jax.random.randint(key_height, (NBX,), NBY - BY // 2, NBY + 1)
    occupancy = jax.random.randint(key_fill, (NBX, NBY), 64, S + 1)
    row_index = jnp.arange(NBY)
    counts = jnp.where(row_index[None, :] < height[:, None], occupancy, 0)
    return jnp.where(row_index[None, :] == 0, S, counts).astype(jnp.int32)


def steps_of(key, dims, shards, low, top_value):
    def one(position, parts):
        heights = jax.random.uniform(jax.random.fold_in(jax.random.fold_in(key, 6), position), (parts,), jnp.float32, low / len(shards), top_value / len(shards))
        return jnp.repeat(jnp.exp(heights), dims[position] // parts).reshape((-1,) + (1,) * (len(dims) - position - 1))

    factor_of = one(*shards[0])
    for cut in shards[1:]:
        factor_of = factor_of * one(*cut)
    return factor_of


def scatter_about(stream_key, shape, scale, limit, cuts=(), held_as=jnp.bfloat16):
    entries = scale * jax.random.normal(stream_key, shape, jnp.float32)
    if cuts:
        entries = entries * steps_of(stream_key, shape, cuts, -0.22, 0.18)
    return jnp.clip(entries, -limit, limit).astype(held_as)


def setup_inputs(seed: int = 0) -> dict:
    keys = jax.random.split(jax.random.key(seed), 5)
    positions = jnp.clip(1.0 * jax.random.uniform(keys[0], (2, NBX, NBY, S), jnp.float32) ** steps_of(keys[0], (2, NBX, NBY, S), ((1, 128), (2, 4)), -0.2, 0.2), 0.0, 1.0)
    velocity = scatter_about(keys[1], (2, NBX, NBY, S), 1.0, 4.0, ((1, 128), (2, 4)), jnp.float32)
    density = draw_density(jax.random.fold_in(keys[4], 71), 0)
    counts = draw_counts(jax.random.fold_in(keys[4], 71), 0)
    return dict(positions=positions, velocity=velocity, density=density, counts=counts)


FAR_SHIFT = 8.0
SOUND_SQ = 100.0
KERNEL_GRAD = 140.0 / math.pi
PARTICLE_MASS = 1.0 / 128.0
GRAVITY = 1.0
TIME_STEP = 0.025

def pack_fields(positions, velocity, density, occupied):
    return jnp.stack([(positions[0] + FAR_SHIFT) * occupied, (positions[1] + FAR_SHIFT) * occupied, velocity[0] * occupied, velocity[1] * occupied, density * occupied])

def column_rates(window):
    bin_rows = window.shape[2] - 2
    centre = window[:, 1, 1:bin_rows + 1]
    centre_pressure = SOUND_SQ * (centre[4] - 1.0)
    force_x = jnp.zeros_like(centre[0])
    force_y = jnp.zeros_like(centre[0])
    compress = jnp.zeros_like(centre[0])
    for offset_col in (-1, 0, 1):
        for offset_row in (-1, 0, 1):
            neighbour = window[:, 1 + offset_col, 1 + offset_row:1 + offset_row + bin_rows]
            delta_x = centre[0][:, :, None] - neighbour[0][:, None, :] - offset_col
            delta_y = centre[1][:, :, None] - neighbour[1][:, None, :] - offset_row
            radius = jnp.sqrt(delta_x * delta_x + delta_y * delta_y)
            weight = jnp.maximum(1.0 - radius, 0.0) ** 3
            pressure = (centre_pressure[:, :, None] + SOUND_SQ * (neighbour[4][:, None, :] - 1.0)) * weight
            force_x = force_x + lax.optimization_barrier(jnp.sum(pressure * delta_x, axis=2))
            force_y = force_y + lax.optimization_barrier(jnp.sum(pressure * delta_y, axis=2))
            closing = (centre[2][:, :, None] - neighbour[2][:, None, :]) * delta_x + (centre[3][:, :, None] - neighbour[3][:, None, :]) * delta_y
            compress = compress + lax.optimization_barrier(jnp.sum(weight * closing, axis=2))
    force_scale = KERNEL_GRAD * PARTICLE_MASS
    return jnp.stack([force_scale * force_x, force_scale * force_y - GRAVITY, -force_scale * compress])

def all_rates(fields):
    padded = jnp.concatenate([fields[:, -1:], fields, fields[:, :1]], axis=1)
    padded = jnp.pad(padded, ((0, 0), (0, 0), (1, 1), (0, 0)))
    columns = jnp.arange(fields.shape[1], dtype=jnp.int32)

    def one_column(column):
        return column_rates(lax.dynamic_slice_in_dim(padded, column, 3, 1))
    per_column = lax.map(one_column, columns)
    return jnp.transpose(per_column, (1, 0, 2, 3))

def reference(positions, velocity, density, counts):
    slot_index = jnp.arange(positions.shape[-1], dtype=jnp.int32)
    occupied = (slot_index[None, None, :] < counts[:, :, None]).astype(jnp.float32)
    fields = pack_fields(positions, velocity, density, occupied)
    first_rates = all_rates(fields)
    half_step = 0.5 * TIME_STEP
    predicted = jnp.stack([fields[0] + half_step * fields[2], fields[1] + half_step * fields[3], fields[2] + half_step * first_rates[0], fields[3] + half_step * first_rates[1], fields[4] + half_step * first_rates[2]]) * occupied
    second_rates = all_rates(predicted)
    final_ux = fields[2] + TIME_STEP * second_rates[0]
    final_uy = fields[3] + TIME_STEP * second_rates[1]
    final_x = fields[0] + half_step * (fields[2] + final_ux) - FAR_SHIFT
    final_y = fields[1] + half_step * (fields[3] + final_uy) - FAR_SHIFT
    final_density = fields[4] + TIME_STEP * second_rates[2]
    new_fields = jnp.stack([final_x, final_y, final_ux, final_uy, final_density]) * occupied
    lowest = jnp.min(jnp.where(occupied > 0.0, final_density, 1000000000.0))
    return (new_fields, lowest)
```

```python
import math

import jax
import jax.numpy as jnp
from jax import lax
from jax.experimental import pallas as pl
from jax.experimental.pallas import tpu as pltpu
from jax.sharding import PartitionSpec as P

SOUND_SQ = 100.0
KERNEL_GRAD = 140.0 / math.pi
PARTICLE_MASS = 1.0 / 128.0
GRAVITY = 1.0
TIME_STEP = 0.025
FORCE_SCALE = KERNEL_GRAD * PARTICLE_MASS
HALF = 0.5 * TIME_STEP

S = 128
NX = 4
NY = 16
HALO = 2
COLS = NX + 2 * HALO
SLOTS = NY + 2 * HALO + 4
BASE = HALO + 2
NB = COLS * SLOTS
GEO = 16
SUMF = 24
FEAT = GEO + SUMF
OFFSETS = ((0, 0), (0, 1), (1, -1), (1, 0), (1, 1))
FAR = 64.0


def split(x, pieces):
    out = []
    for _ in range(pieces - 1):
        h = x.astype(jnp.bfloat16).astype(jnp.float32)
        out.append(h)
        x = x - h
    out.append(x)
    return out


def grid_coords():
    row = lax.broadcasted_iota(jnp.int32, (NB, S), 0)
    col = (row * 171) >> 12
    slot = row - col * SLOTS
    cx = col.astype(jnp.float32) - 0.5 * (COLS - 1)
    cy = slot.astype(jnp.float32) - 0.5 * (SLOTS - 1)
    return cx, cy


def build(x, y, u, v, rho, occ, feat_ref, geo_ref, comb_ref, acc_ref):
    def put(ref, width, f, val):
        ref[pl.ds(f, NB, stride=width), :] = val

    zero = jnp.zeros((NB, S), jnp.float32)
    one = jnp.ones((NB, S), jnp.float32)
    off = (1.0 - occ) * FAR
    xs = split(x, 2)
    ys = split(y, 2)
    xt = xs[0] + xs[1].astype(jnp.bfloat16).astype(jnp.float32)
    yt = ys[0] + ys[1].astype(jnp.bfloat16).astype(jnp.float32)
    rr = split(xt * xt + yt * yt + off, 3)
    rows = [xs[0], xs[0], xs[1], xs[1], ys[0], ys[0], ys[1], ys[1], *rr, one, one, one]
    cx, cy = grid_coords()
    gx = cx + x
    gy = cy + y
    p = SOUND_SQ * (rho - 1.0) * occ
    rows += [zero, zero]
    rows += [one]
    rows += split(gx, 3) + split(gy, 3) + split(p, 2) + split(p * gx, 3) + split(p * gy, 3)
    rows += split(u, 2) + split(v, 2) + split(u * gx + v * gy, 3)
    rows += [zero] * (FEAT - len(rows))
    for f, val in enumerate(rows):
        put(feat_ref, FEAT, f, val)
    for k, (dx, dy) in enumerate(OFFSETS):
        bx = x + dx
        by = y + dy
        hx = split(bx, 2)
        hy = split(by, 2)
        tx = hx[0] + hx[1].astype(jnp.bfloat16).astype(jnp.float32)
        ty = hy[0] + hy[1].astype(jnp.bfloat16).astype(jnp.float32)
        nn = split(tx * tx + ty * ty + off, 3)
        g = [-2.0 * hx[0], -2.0 * hx[1], -2.0 * hx[0], -2.0 * hx[1]]
        g += [-2.0 * hy[0], -2.0 * hy[1], -2.0 * hy[0], -2.0 * hy[1]]
        g += [one, one, one, *nn, zero, zero]
        for f, val in enumerate(g):
            geo_ref[pl.ds(k * NB * GEO + f, NB, stride=GEO), :] = val

    def turn(r, carry):
        block = feat_ref[pl.ds(pl.multiple_of(r * FEAT, 8), FEAT), :]
        comb_ref[r] = block.T.astype(jnp.bfloat16)
        return carry

    lax.fori_loop(0, NB, turn, 0, unroll=4)
    acc_ref[...] = jnp.zeros_like(acc_ref)


def interact(a, ks, fine, feat_ref, geo_ref, comb_ref, acc_ref):
    bins = [a + OFFSETS[k][0] * SLOTS + OFFSETS[k][1] for k in ks]
    lhs = comb_ref[a][:, :GEO]
    g = jnp.concatenate(
        [geo_ref[pl.ds(pl.multiple_of((k * NB + b) * GEO, 8), GEO), :] for k, b in zip(ks, bins)], axis=1
    ).astype(jnp.bfloat16)
    r2 = jnp.dot(lhs, g, preferred_element_type=jnp.float32)
    t = jnp.maximum(r2, 1e-30)
    q = jnp.maximum(1.0 - t * lax.rsqrt(t), 0.0)
    w = q * q * q
    parts = [w.astype(jnp.bfloat16)]
    if fine:
        parts.append((w - parts[0].astype(jnp.float32)).astype(jnp.bfloat16))
    right = jnp.concatenate([comb_ref[b] for b in bins], axis=0)
    left = feat_ref[pl.ds(pl.multiple_of(a * FEAT + GEO, 8), SUMF), :].astype(jnp.bfloat16)
    to_a = sum(jnp.dot(w_, right, preferred_element_type=jnp.float32) for w_ in parts)
    to_b = sum(jnp.dot(left, w_, preferred_element_type=jnp.float32) for w_ in parts)
    at = pl.ds(pl.multiple_of(a * SUMF, 8), SUMF)
    acc_ref[at, :] = acc_ref[at, :] + to_a.T[GEO:FEAT]
    for n, (k, b) in enumerate(zip(ks, bins)):
        if k == 0:
            continue
        at = pl.ds(pl.multiple_of(b * SUMF, 8), SUMF)
        acc_ref[at, :] = acc_ref[at, :] + to_b[:, n * S : (n + 1) * S]


def sweep(ring, fine, refs):
    c0, c1 = ring + 1, COLS - 2 - ring
    s0, s1 = ring + 3, SLOTS - 4 - ring

    def column(c, carry):
        def row(s, carry):
            interact(c * SLOTS + s, (0, 1, 2, 3, 4), fine, *refs)
            return carry

        return lax.fori_loop(s0 - 1, s1 + 1, row, carry)

    lax.fori_loop(c0, c1 + 1, column, 0)

    def rim(t, carry):
        n = s1 - s0 + 3
        a = jnp.where(t < n, (c0 - 1) * SLOTS + s0 - 1 + t, (c0 + t - n) * SLOTS + s1 + 1)
        interact(a, (2, 3, 4), fine, *refs)
        return carry

    lax.fori_loop(0, s1 - s0 + 3 + c1 - c0, rim, 0)


def gather_rates(x, y, u, v, rho, occ, acc_ref):
    def get(f):
        return acc_ref[pl.ds(f, NB, stride=SUMF), :]

    cx, cy = grid_coords()
    gx = cx + x
    gy = cy + y
    p = SOUND_SQ * (rho - 1.0) * occ
    s1 = get(0)
    sx = get(1) + (get(2) + get(3))
    sy = get(4) + (get(5) + get(6))
    sp = get(7) + get(8)
    spx = get(9) + (get(10) + get(11))
    spy = get(12) + (get(13) + get(14))
    su = get(15) + get(16)
    sv = get(17) + get(18)
    se = get(19) + (get(20) + get(21))
    dx = gx * s1 - sx
    dy = gy * s1 - sy
    fx = p * dx + (gx * sp - spx)
    fy = p * dy + (gy * sp - spy)
    comp = u * dx + v * dy - (gx * su + gy * sv - se)
    return FORCE_SCALE * fx, FORCE_SCALE * fy - GRAVITY, -FORCE_SCALE * comp


def step_kernel(ext_ref, new_ref, low_ref, feat_ref, geo_ref, comb_ref, acc_ref):
    refs = (feat_ref, geo_ref, comb_ref, acc_ref)

    def load():
        rho = ext_ref[4]
        occ = jnp.where(rho > 0.0, 1.0, 0.0)
        x = (ext_ref[0] - 0.5) * occ
        y = (ext_ref[1] - 0.5) * occ
        return x, y, ext_ref[2] * occ, ext_ref[3] * occ, rho, occ

    x, y, u, v, rho, occ = load()
    build(x, y, u, v, rho, occ, *refs)
    sweep(0, False, refs)
    x, y, u, v, rho, occ = load()
    ax, ay, ar = gather_rates(x, y, u, v, rho, occ, acc_ref)

    def predicted():
        return (
            (x + HALF * u) * occ,
            (y + HALF * v) * occ,
            (u + HALF * ax) * occ,
            (v + HALF * ay) * occ,
            (rho + HALF * ar) * occ,
        )

    px, py, pu, pv, pr = predicted()
    build(px, py, pu, pv, pr, occ, *refs)
    sweep(1, True, refs)
    ax, ay, ar = gather_rates(px, py, pu, pv, pr, occ, acc_ref)
    x, y, u, v, rho, occ = load()
    nu = u + TIME_STEP * ax
    nv = v + TIME_STEP * ay
    nx = ext_ref[0] + HALF * (u + nu)
    ny = ext_ref[1] + HALF * (v + nv)
    nr = rho + TIME_STEP * ar
    low = jnp.where(occ > 0.0, nr, 1000000000.0)
    lows = []
    for c in range(NX):
        at = slice((c + HALO) * SLOTS + BASE, (c + HALO) * SLOTS + BASE + NY)
        for f, val in enumerate((nx, ny, nu, nv, nr)):
            new_ref[f, c] = jnp.where(occ[at] > 0.0, val[at], 0.0)
        lows.append(low[at])
    low_ref[...] = jnp.min(jnp.concatenate(lows, axis=0), axis=0, keepdims=True)


def sph_step(ext):
    return pl.pallas_call(
        step_kernel,
        out_shape=(
            jax.ShapeDtypeStruct((5, NX, NY, S), jnp.float32),
            jax.ShapeDtypeStruct((1, S), jnp.float32),
        ),
        in_specs=[pl.BlockSpec(memory_space=pltpu.VMEM)],
        out_specs=(
            pl.BlockSpec(memory_space=pltpu.VMEM),
            pl.BlockSpec(memory_space=pltpu.VMEM),
        ),
        scratch_shapes=[
            pltpu.VMEM((NB * FEAT, S), jnp.float32),
            pltpu.VMEM((len(OFFSETS) * NB * GEO, S), jnp.float32),
            pltpu.VMEM((NB, S, FEAT), jnp.bfloat16),
            pltpu.VMEM((NB * SUMF, S), jnp.float32),
        ],
        name="sph_step",
    )(ext)


def padded(x, axis, dim, width, wrap):
    size, length = lax.axis_size(axis), x.shape[dim]
    up = [(i, (i + 1) % size) for i in range(size if wrap else size - 1)]
    down = [(j, i) for i, j in up]
    last = lax.slice_in_dim(x, length - width, length, axis=dim)
    leading = lax.slice_in_dim(x, 0, width, axis=dim)
    before = lax.ppermute(last, axis, up)
    after = lax.ppermute(leading, axis, down)
    return jnp.concatenate([before, x, after], axis=dim)


def body(positions, velocity, density, counts):
    slot_index = jnp.arange(S, dtype=jnp.int32)
    rho = jnp.where(slot_index[None, None, :] < counts[:, :, None], density, 0.0)
    fields = jnp.concatenate([positions, velocity, rho[None]], axis=0)
    ext = padded(fields, "chan", 1, HALO, True)
    ext = padded(ext, "cross", 2, HALO, False)
    ext = jnp.pad(ext, ((0, 0), (0, 0), (BASE - HALO, SLOTS - NY - HALO - BASE), (0, 0)))
    new_fields, low = sph_step(ext.reshape(5, NB, S))
    own = jnp.broadcast_to(jnp.min(low), (lax.axis_size("chan") * lax.axis_size("cross"), S))
    everyone = lax.all_to_all(own, ("chan", "cross"), 0, 0, tiled=True)
    return (new_fields, jnp.min(everyone))


def solution(mesh):
    return jax.shard_map(
        body,
        mesh=mesh,
        in_specs=(
            P(None, "chan", "cross", None),
            P(None, "chan", "cross", None),
            P("chan", "cross", None),
            P("chan", "cross"),
        ),
        out_specs=(P(None, "chan", "cross", None), P()),
        check_vma=False,
    )
```

```python
import math

import jax
import jax.numpy as jnp
from jax import lax
from jax.experimental import pallas as pl
from jax.experimental.pallas import tpu as pltpu
from jax.sharding import PartitionSpec as P

SOUND_SQ = 100.0
KERNEL_GRAD = 140.0 / math.pi
PARTICLE_MASS = 1.0 / 128.0
GRAVITY = 1.0
TIME_STEP = 0.025
FORCE_SCALE = KERNEL_GRAD * PARTICLE_MASS
HALF = 0.5 * TIME_STEP

S = 128
NX = 4
NY = 16
HALO = 2
COLS = NX + 2 * HALO
SLOTS = NY + 2 * HALO + 4
BASE = HALO + 2
NB = COLS * SLOTS
SUMF = 24
TALL = 32
OFFSETS = ((0, 0), (0, 1), (1, -1), (1, 0), (1, 1))
FAR = 1000.0
PLANE = 32


def split(x, pieces):
    out = []
    for _ in range(pieces - 1):
        h = x.astype(jnp.bfloat16).astype(jnp.float32)
        out.append(h)
        x = x - h
    out.append(x)
    return out


def on_grid(x, y):
    row = lax.broadcasted_iota(jnp.int32, (NB, S), 0)
    col = (row * 171) >> 12
    slot = row - col * SLOTS
    return (
        x + (col.astype(jnp.float32) - 0.5 * (COLS - 1)),
        y + (slot.astype(jnp.float32) - 0.5 * (SLOTS - 1)),
    )


def build(x, y, u, v, rho, occ, direct, refs):
    plane_ref, turned_ref, gx_ref, gy_ref, p_ref, u_ref, v_ref, acc_ref = refs
    acc_ref[...] = jnp.zeros_like(acc_ref)
    gx, gy = on_grid(x, y)
    gx_ref[...] = jnp.where(occ > 0.0, gx, FAR)
    gy_ref[...] = gy
    p = SOUND_SQ * (rho - 1.0) * occ
    if direct:
        p_ref[...] = p
        u_ref[...] = u
        v_ref[...] = v
        return
    gx = gx * occ
    gy = gy * occ
    rows = [occ] + split(gx, 3) + split(gy, 3) + split(u, 2) + split(v, 2) + split(u * gx + v * gy, 3)
    rows += split(p, 2) + split(p * gx, 3) + split(p * gy, 3)
    rows += [jnp.zeros((NB, S), jnp.float32)] * (SUMF - len(rows))
    for f, val in enumerate(rows):
        plane_ref[f * NB : (f + 1) * NB, :] = val

    def turn(r, carry):
        block = plane_ref[pl.ds(r, SUMF, stride=NB), :]
        block = jnp.concatenate([block, jnp.zeros((TALL - SUMF, S), jnp.float32)], axis=0)
        turned_ref[r] = block.astype(jnp.bfloat16)
        return carry

    lax.fori_loop(0, NB, turn, 0, unroll=8)


def geometry(a, bins, refs):
    gx_ref, gy_ref = refs[2], refs[3]
    ax = down(gx_ref, a)
    ay = down(gy_ref, a)
    for b in bins:
        dx = ax - gx_ref[pl.ds(b, 1), :]
        dy = ay - gy_ref[pl.ds(b, 1), :]
        t = jnp.maximum(dx * dx + dy * dy, 1e-30)
        q = jnp.maximum(1.0 - t * lax.rsqrt(t), 0.0)
        yield b, dx, dy, q * q * q


def down(ref, a):
    return jnp.broadcast_to(ref[pl.ds(a, 1), :], (S, S)).T


def pair_sums(a, ks, direct, refs):
    bins = [a + OFFSETS[k][0] * SLOTS + OFFSETS[k][1] for k in ks]
    if direct:
        return direct_sums(a, bins, ks, refs)
    turned_ref = refs[1]
    w = jnp.concatenate([w.astype(jnp.bfloat16) for _, _, _, w in geometry(a, bins, refs)], axis=1)
    right = jnp.concatenate([turned_ref[b] for b in bins], axis=1)
    to_a = lax.dot_general(right, w, (((1,), (1,)), ((), ())), preferred_element_type=jnp.float32)
    to_b = jnp.dot(turned_ref[a], w, preferred_element_type=jnp.float32)
    out = [(a, to_a[:SUMF])]
    for n, (k, b) in enumerate(zip(ks, bins)):
        if k != 0:
            out.append((b, to_b[:SUMF, n * S : (n + 1) * S]))
    return out


def direct_sums(a, bins, ks, refs):
    p_ref, u_ref, v_ref = refs[4:7]
    ap, au, av = (down(ref, a) for ref in (p_ref, u_ref, v_ref))
    rows = None
    out = []
    fill = jnp.zeros((8 - 3, S), jnp.float32)
    for k, (b, dx, dy, w) in zip(ks, geometry(a, bins, refs)):
        at = pl.ds(b, 1)
        wx = w * dx
        wy = w * dy
        p = ap + p_ref[at, :]
        vals = (p * wx, p * wy, (au - u_ref[at, :]) * wx + (av - v_ref[at, :]) * wy)
        rows = vals if rows is None else tuple(r + x for r, x in zip(rows, vals))
        if k != 0:
            fx, fy, co = (jnp.sum(x, axis=0, keepdims=True) for x in vals)
            out.append((b, jnp.concatenate([-fx, -fy, co, fill], axis=0)))
    rows = [jnp.sum(r.T, axis=0, keepdims=True) for r in rows]
    out.append((a, jnp.concatenate([*rows, fill], axis=0)))
    return out


def interact(many, ks, direct, refs):
    acc_ref = refs[-1]
    sums = [pair_sums(a, ks, direct, refs) for a in many]
    for group in sums:
        for b, val in group:
            at = pl.ds(pl.multiple_of(b * SUMF, 8), val.shape[0])
            acc_ref[at, :] = acc_ref[at, :] + val


def sweep(ring, direct, many, refs):
    c0, c1 = ring + 1, COLS - 2 - ring
    s0, s1 = ring + 3, SLOTS - 4 - ring
    step = (c1 - c0 + 1) // many

    def column(c, carry):
        def row(s, carry):
            interact([(c + step * m) * SLOTS + s for m in range(many)], (0, 1, 2, 3, 4), direct, refs)
            return carry

        return lax.fori_loop(s0 - 1, s1 + 1, row, carry)

    lax.fori_loop(c0, c0 + step, column, 0)
    n = s1 - s0 + 3
    total = n + c1 - c0
    group = 5 if total % 5 == 0 else 3 if total % 3 == 0 else 1

    def rim(i, carry):
        ts = [i * group + m for m in range(group)]
        at = [jnp.where(t < n, (c0 - 1) * SLOTS + s0 - 1 + t, (c0 + t - n) * SLOTS + s1 + 1) for t in ts]
        interact(at, (2, 3, 4), direct, refs)
        return carry

    lax.fori_loop(0, total // group, rim, 0)


def gather_rates(x, y, u, v, rho, occ, direct, acc_ref):
    def get(f):
        return acc_ref[pl.ds(f, NB, stride=SUMF), :]

    if direct:
        fx, fy, comp = get(0), get(1), get(2)
    else:
        gx, gy = on_grid(x, y)
        s1 = get(0)
        dx = gx * s1 - (get(1) + (get(2) + get(3)))
        dy = gy * s1 - (get(4) + (get(5) + get(6)))
        se = get(11) + (get(12) + get(13))
        comp = u * dx + v * dy - (gx * (get(7) + get(8)) + gy * (get(9) + get(10)) - se)
        p = SOUND_SQ * (rho - 1.0) * occ
        sp = get(14) + get(15)
        fx = p * dx + (gx * sp - (get(16) + (get(17) + get(18))))
        fy = p * dy + (gy * sp - (get(19) + (get(20) + get(21))))
    return FORCE_SCALE * fx, FORCE_SCALE * fy - GRAVITY, -FORCE_SCALE * comp


def step_kernel(ext_ref, new_ref, low_ref, *refs):
    acc_ref = refs[-1]

    def load():
        rho = ext_ref[4]
        occ = jnp.where(rho > 0.0, 1.0, 0.0)
        x = (ext_ref[0] - 0.5) * occ
        y = (ext_ref[1] - 0.5) * occ
        return x, y, ext_ref[2] * occ, ext_ref[3] * occ, rho, occ

    x, y, u, v, rho, occ = load()
    build(x, y, u, v, rho, occ, False, refs)
    sweep(0, False, 3, refs)
    x, y, u, v, rho, occ = load()
    ax, ay, ar = gather_rates(x, y, u, v, rho, occ, False, acc_ref)

    def predicted():
        return (
            (x + HALF * u) * occ,
            (y + HALF * v) * occ,
            (u + HALF * ax) * occ,
            (v + HALF * ay) * occ,
            (rho + HALF * ar) * occ,
        )

    px, py, pu, pv, pr = predicted()
    build(px, py, pu, pv, pr, occ, True, refs)
    sweep(1, True, 2, refs)
    ax, ay, ar = gather_rates(px, py, pu, pv, pr, occ, True, acc_ref)
    x, y, u, v, rho, occ = load()
    nu = u + TIME_STEP * ax
    nv = v + TIME_STEP * ay
    nx = ext_ref[0] + HALF * (u + nu)
    ny = ext_ref[1] + HALF * (v + nv)
    nr = rho + TIME_STEP * ar
    low = jnp.where(occ > 0.0, nr, 1000000000.0)
    lows = []
    for c in range(NX):
        at = slice((c + HALO) * SLOTS + BASE, (c + HALO) * SLOTS + BASE + NY)
        for f, val in enumerate((nx, ny, nu, nv, nr)):
            new_ref[f, c] = jnp.where(occ[at] > 0.0, val[at], 0.0)
        lows.append(low[at])
    low_ref[...] = jnp.broadcast_to(jnp.min(jnp.concatenate(lows, axis=0)), low_ref.shape)


def sph_step(ext):
    return pl.pallas_call(
        step_kernel,
        out_shape=(
            jax.ShapeDtypeStruct((5, NX, NY, S), jnp.float32),
            jax.ShapeDtypeStruct((PLANE, S), jnp.float32),
        ),
        in_specs=[pl.BlockSpec(memory_space=pltpu.VMEM)],
        out_specs=(
            pl.BlockSpec(memory_space=pltpu.VMEM),
            pl.BlockSpec(memory_space=pltpu.VMEM),
        ),
        scratch_shapes=[
            pltpu.VMEM((SUMF * NB, S), jnp.float32),
            pltpu.VMEM((NB, TALL, S), jnp.bfloat16),
            pltpu.VMEM((NB, S), jnp.float32),
            pltpu.VMEM((NB, S), jnp.float32),
            pltpu.VMEM((NB, S), jnp.float32),
            pltpu.VMEM((NB, S), jnp.float32),
            pltpu.VMEM((NB, S), jnp.float32),
            pltpu.VMEM((NB * SUMF, S), jnp.float32),
        ],
        name="sph_step",
    )(ext)


def swap(x, dim, axis, wrap):
    size, length = lax.axis_size(axis), x.shape[dim]
    even = lax.axis_index(axis) % 2 == 0
    last = lax.slice_in_dim(x, length - HALO, length, axis=dim)
    first = lax.slice_in_dim(x, 0, HALO, axis=dim)

    def pairs(start):
        ends = [(i, (i + 1) % size) for i in range(start, size if wrap else size - 1, 2)]
        return ends + [(j, i) for i, j in ends]

    near = lax.ppermute(jnp.where(even, last, first), axis, pairs(0))
    far = lax.ppermute(jnp.where(even, first, last), axis, pairs(1))
    return jnp.where(even, far, near), jnp.where(even, near, far)


def minimum_everywhere(low):
    chan, cross = lax.axis_size("chan"), lax.axis_size("cross")
    planes = {}
    for i in range(chan * cross):
        planes.setdefault((i // cross // 4 % 8, i % cross // 2), []).append(i)
    planes = list(planes.values())
    lines = [list(line) for line in zip(*planes)]
    both = ("chan", "cross")
    got = lax.all_to_all(low, both, 0, 0, tiled=True, axis_index_groups=planes)
    got = jnp.broadcast_to(jnp.min(got, axis=0, keepdims=True), (len(planes), S))
    return jnp.min(lax.all_to_all(got, both, 0, 0, tiled=True, axis_index_groups=lines))


def body(positions, velocity, density, counts):
    slot_index = jnp.arange(S, dtype=jnp.int32)
    rho = jnp.where(slot_index[None, None, :] < counts[:, :, None], density, 0.0)
    fields = jnp.concatenate([positions, velocity, rho[None]], axis=0)
    before, after = swap(fields, 1, "chan", True)
    wide = jnp.concatenate([before, fields, after], axis=1)
    below, above = swap(wide, 2, "cross", False)
    ext = jnp.concatenate([below, wide, above], axis=2)
    ext = jnp.pad(ext, ((0, 0), (0, 0), (BASE - HALO, SLOTS - NY - HALO - BASE), (0, 0)))
    new_fields, low = sph_step(ext.reshape(5, NB, S))
    return (new_fields, minimum_everywhere(low))


def solution(mesh):
    return jax.shard_map(
        body,
        mesh=mesh,
        in_specs=(
            P(None, "chan", "cross", None),
            P(None, "chan", "cross", None),
            P("chan", "cross", None),
            P("chan", "cross"),
        ),
        out_specs=(P(None, "chan", "cross", None), P()),
        check_vma=False,
    )
```

```python
import math

import jax
import jax.numpy as jnp
from jax import lax
from jax.experimental import pallas as pl
from jax.experimental.pallas import tpu as pltpu
from jax.sharding import PartitionSpec as P

SOUND_SQ = 100.0
KERNEL_GRAD = 140.0 / math.pi
PARTICLE_MASS = 1.0 / 128.0
GRAVITY = 1.0
TIME_STEP = 0.025
FORCE_SCALE = KERNEL_GRAD * PARTICLE_MASS
HALF = 0.5 * TIME_STEP

S = 128
NX = 4
NY = 16
HALO = 2
COLS = NX + 2 * HALO
SLOTS = NY + 2 * HALO + 4
BASE = HALO + 2
NB = COLS * SLOTS
SUMF = 24
WIDTH = SUMF + 8
TALL = 32
OFFSETS = ((0, 0), (0, 1), (1, -1), (1, 0), (1, 1))
DIRECT = (0, 1)
CHAIN = 2
FAR = 1000.0
PLANE = 32


def split(x, pieces):
    out = []
    for _ in range(pieces - 1):
        h = x.astype(jnp.bfloat16).astype(jnp.float32)
        out.append(h)
        x = x - h
    out.append(x)
    return out


def on_grid(x, y):
    row = lax.broadcasted_iota(jnp.int32, (NB, S), 0)
    col = (row * 171) >> 12
    slot = row - col * SLOTS
    return (
        x + (col.astype(jnp.float32) - 0.5 * (COLS - 1)),
        y + (slot.astype(jnp.float32) - 0.5 * (SLOTS - 1)),
    )


def build(x, y, u, v, rho, occ, low, high, refs):
    plane_ref, turned_ref, gx_ref, gy_ref, p_ref, u_ref, v_ref, acc_ref = refs
    acc_ref[...] = jnp.zeros_like(acc_ref)
    gx, gy = on_grid(x, y)
    gx_ref[...] = jnp.where(occ > 0.0, gx, FAR)
    gy_ref[...] = gy
    p = SOUND_SQ * (rho - 1.0) * occ
    p_ref[...] = p
    u_ref[...] = u
    v_ref[...] = v
    gx = gx * occ
    gy = gy * occ
    rows = [occ] + split(gx, 3) + split(gy, 3) + split(u, 2) + split(v, 2) + split(u * gx + v * gy, 3)
    rows += split(p, 2) + split(p * gx, 3) + split(p * gy, 3)
    rows += [jnp.zeros((NB, S), jnp.float32)] * (SUMF - len(rows))
    for f, val in enumerate(rows):
        plane_ref[f * NB : (f + 1) * NB, :] = val

    def turn(r, carry):
        block = plane_ref[pl.ds(r, SUMF, stride=NB), :]
        block = jnp.concatenate([block, jnp.zeros((TALL - SUMF, S), jnp.float32)], axis=0)
        turned_ref[r] = block.astype(jnp.bfloat16)
        return carry

    lax.fori_loop(low, high, turn, 0, unroll=8)


def geometry(a, bins, refs):
    gx_ref, gy_ref = refs[2], refs[3]
    ax = down(gx_ref, a)
    ay = down(gy_ref, a)
    for b in bins:
        dx = ax - gx_ref[pl.ds(b, 1), :]
        dy = ay - gy_ref[pl.ds(b, 1), :]
        t = jnp.maximum(dx * dx + dy * dy, 1e-30)
        q = jnp.maximum(1.0 - t * lax.rsqrt(t), 0.0)
        yield b, dx, dy, q * q * q


def down(ref, a):
    return jnp.broadcast_to(ref[pl.ds(a, 1), :], (S, S)).T


def column_sums(chain, ks, fine, refs):
    turned_ref = refs[1]
    direct = DIRECT if fine else ()
    p_ref, u_ref, v_ref = refs[4:7]
    out = []
    tiles = []
    for a in chain:
        bins = [a + OFFSETS[k][0] * SLOTS + OFFSETS[k][1] for k in ks]
        rows = []
        mine = {}
        for k, (b, dx, dy, w) in zip(ks, geometry(a, bins, refs)):
            if k not in direct:
                mine[k] = [w.astype(jnp.bfloat16)]
                if fine:
                    mine[k].append((w - mine[k][0].astype(jnp.float32)).astype(jnp.bfloat16))
                continue
            if not rows:
                ap, au, av = (down(ref, a) for ref in (p_ref, u_ref, v_ref))
            at = pl.ds(b, 1)
            wx = w * dx
            wy = w * dy
            p = ap + p_ref[at, :]
            vals = (p * wx, p * wy, (au - u_ref[at, :]) * wx + (av - v_ref[at, :]) * wy)
            rows = [r + x for r, x in zip(rows, vals)] if rows else list(vals)
            if k != 0:
                fx, fy, co = (jnp.sum(x, axis=0, keepdims=True) for x in vals)
                out.append((b * WIDTH + SUMF, fill_rows(-fx, -fy, co)))
        if rows:
            rows = [jnp.sum(r.T, axis=0, keepdims=True) for r in rows]
            out.append((a * WIDTH + SUMF, fill_rows(*rows)))
        tiles.append(mine)
        others = [k for k in mine if k != 0]
        to_b = sum(
            jnp.dot(turned_ref[a], jnp.concatenate([mine[k][n] for k in others], axis=1), preferred_element_type=jnp.float32)
            for n in range(2 if fine else 1)
        )
        for n, k in enumerate(others):
            b = a + OFFSETS[k][0] * SLOTS + OFFSETS[k][1]
            out.append((b * WIDTH, to_b[:SUMF, n * S : (n + 1) * S]))
    base = chain[0]
    partners = sorted({(OFFSETS[k][0], OFFSETS[k][1] + m) for m, mine in enumerate(tiles) for k in mine})
    right = jnp.concatenate([turned_ref[base + i * SLOTS + j] for i, j in partners], axis=1)
    none = jnp.zeros((S, S), jnp.bfloat16)
    to_a = 0.0
    for n in range(2 if fine else 1):
        w = []
        for m, mine in enumerate(tiles):
            at = {(OFFSETS[k][0], OFFSETS[k][1] + m): mine[k][n] for k in mine}
            w.append(jnp.concatenate([at.get(ij, none) for ij in partners], axis=1))
        w = jnp.concatenate(w, axis=0)
        to_a = to_a + lax.dot_general(right, w, (((1,), (1,)), ((), ())), preferred_element_type=jnp.float32)
    for m, a in enumerate(chain):
        out.append((a * WIDTH, to_a[:SUMF, m * S : (m + 1) * S]))
    return out


def fill_rows(*rows):
    return jnp.concatenate([*rows, jnp.zeros((8 - len(rows), S), jnp.float32)], axis=0)


def interact(many, ks, fine, refs):
    acc_ref = refs[-1]
    sums = [column_sums(chain, ks, fine, refs) for chain in many]
    for group in sums:
        for row, val in group:
            at = pl.ds(pl.multiple_of(row, 8), val.shape[0])
            acc_ref[at, :] = acc_ref[at, :] + val


def sweep(ring, fine, many, refs):
    c0, c1 = ring + 1, COLS - 2 - ring
    s0, s1 = ring + 3, SLOTS - 4 - ring
    wide, tall = c1 - c0 + 1, s1 - s0 + 1
    step = wide // many

    def column(c, carry):
        def row(t, carry):
            a = c * SLOTS + s0 + CHAIN * t
            interact([[a + step * m * SLOTS + n for n in range(CHAIN)] for m in range(many)], (0, 1, 2, 3, 4), fine, refs)
            return carry

        return lax.fori_loop(0, tall // CHAIN, row, carry)

    lax.fori_loop(c0, c0 + step, column, 0)

    def bottom(t, carry):
        interact([[(c0 + 2 * t + m) * SLOTS + s0 - 1] for m in range(2)], (1, 4), fine, refs)
        return carry

    lax.fori_loop(0, wide // 2, bottom, 0)
    n = tall + 2
    total = n + wide - 1
    group = 5 if total % 5 == 0 else 7 if total % 7 == 0 else 1

    def rim(i, carry):
        ts = [i * group + m for m in range(group)]
        at = [jnp.where(t < n, (c0 - 1) * SLOTS + s0 - 1 + t, (c0 + t - n) * SLOTS + s1 + 1) for t in ts]
        interact([[a] for a in at], (2, 3, 4), fine, refs)
        return carry

    lax.fori_loop(0, total // group, rim, 0)


def gather_rates(x, y, u, v, rho, occ, fine, acc_ref):
    def get(f):
        return acc_ref[pl.ds(f, NB, stride=WIDTH), :]

    gx, gy = on_grid(x, y)
    s1 = get(0)
    dx = gx * s1 - (get(1) + (get(2) + get(3)))
    dy = gy * s1 - (get(4) + (get(5) + get(6)))
    se = get(11) + (get(12) + get(13))
    comp = u * dx + v * dy - (gx * (get(7) + get(8)) + gy * (get(9) + get(10)) - se)
    p = SOUND_SQ * (rho - 1.0) * occ
    sp = get(14) + get(15)
    fx = p * dx + (gx * sp - (get(16) + (get(17) + get(18))))
    fy = p * dy + (gy * sp - (get(19) + (get(20) + get(21))))
    if fine:
        fx = fx + get(SUMF)
        fy = fy + get(SUMF + 1)
        comp = comp + get(SUMF + 2)
    return FORCE_SCALE * fx, FORCE_SCALE * fy - GRAVITY, -FORCE_SCALE * comp


def step_kernel(ext_ref, new_ref, low_ref, *refs):
    acc_ref = refs[-1]

    def load():
        rho = ext_ref[4]
        occ = jnp.where(rho > 0.0, 1.0, 0.0)
        x = (ext_ref[0] - 0.5) * occ
        y = (ext_ref[1] - 0.5) * occ
        return x, y, ext_ref[2] * occ, ext_ref[3] * occ, rho, occ

    x, y, u, v, rho, occ = load()
    build(x, y, u, v, rho, occ, 0, NB, refs)
    sweep(0, False, 6, refs)
    x, y, u, v, rho, occ = load()
    ax, ay, ar = gather_rates(x, y, u, v, rho, occ, False, acc_ref)

    def predicted():
        return (
            (x + HALF * u) * occ,
            (y + HALF * v) * occ,
            (u + HALF * ax) * occ,
            (v + HALF * ay) * occ,
            (rho + HALF * ar) * occ,
        )

    px, py, pu, pv, pr = predicted()
    build(px, py, pu, pv, pr, occ, SLOTS, NB - SLOTS, refs)
    sweep(1, True, 4, refs)
    ax, ay, ar = gather_rates(px, py, pu, pv, pr, occ, True, acc_ref)
    x, y, u, v, rho, occ = load()
    nu = u + TIME_STEP * ax
    nv = v + TIME_STEP * ay
    nx = ext_ref[0] + HALF * (u + nu)
    ny = ext_ref[1] + HALF * (v + nv)
    nr = rho + TIME_STEP * ar
    low = jnp.where(occ > 0.0, nr, 1000000000.0)
    lows = []
    for c in range(NX):
        at = slice((c + HALO) * SLOTS + BASE, (c + HALO) * SLOTS + BASE + NY)
        for f, val in enumerate((nx, ny, nu, nv, nr)):
            new_ref[f, c] = jnp.where(occ[at] > 0.0, val[at], 0.0)
        lows.append(low[at])
    low_ref[...] = jnp.broadcast_to(jnp.min(jnp.concatenate(lows, axis=0)), low_ref.shape)


def sph_step(ext):
    return pl.pallas_call(
        step_kernel,
        out_shape=(
            jax.ShapeDtypeStruct((5, NX, NY, S), jnp.float32),
            jax.ShapeDtypeStruct((PLANE, S), jnp.float32),
        ),
        in_specs=[pl.BlockSpec(memory_space=pltpu.VMEM)],
        out_specs=(
            pl.BlockSpec(memory_space=pltpu.VMEM),
            pl.BlockSpec(memory_space=pltpu.VMEM),
        ),
        scratch_shapes=[
            pltpu.VMEM((SUMF * NB, S), jnp.float32),
            pltpu.VMEM((NB, TALL, S), jnp.bfloat16),
            pltpu.VMEM((NB, S), jnp.float32),
            pltpu.VMEM((NB, S), jnp.float32),
            pltpu.VMEM((NB, S), jnp.float32),
            pltpu.VMEM((NB, S), jnp.float32),
            pltpu.VMEM((NB, S), jnp.float32),
            pltpu.VMEM((NB * WIDTH, S), jnp.float32),
        ],
        name="sph_step",
    )(ext)


def swap(x, dim, axis, wrap):
    size, length = lax.axis_size(axis), x.shape[dim]
    even = lax.axis_index(axis) % 2 == 0
    last = lax.slice_in_dim(x, length - HALO, length, axis=dim)
    first = lax.slice_in_dim(x, 0, HALO, axis=dim)

    def pairs(start):
        ends = [(i, (i + 1) % size) for i in range(start, size if wrap else size - 1, 2)]
        return ends + [(j, i) for i, j in ends]

    near = lax.ppermute(jnp.where(even, last, first), axis, pairs(0))
    far = lax.ppermute(jnp.where(even, first, last), axis, pairs(1))
    return jnp.where(even, far, near), jnp.where(even, near, far)


def minimum_everywhere(low):
    chan, cross = lax.axis_size("chan"), lax.axis_size("cross")
    planes = {}
    for i in range(chan * cross):
        planes.setdefault((i // cross // 4 % 8, i % cross // 2), []).append(i)
    planes = list(planes.values())
    lines = [list(line) for line in zip(*planes)]
    both = ("chan", "cross")
    got = lax.all_to_all(low, both, 0, 0, tiled=True, axis_index_groups=planes)
    got = jnp.broadcast_to(jnp.min(got, axis=0, keepdims=True), (len(planes), S))
    return jnp.min(lax.all_to_all(got, both, 0, 0, tiled=True, axis_index_groups=lines))


def body(positions, velocity, density, counts):
    slot_index = jnp.arange(S, dtype=jnp.int32)
    rho = jnp.where(slot_index[None, None, :] < counts[:, :, None], density, 0.0)
    fields = jnp.concatenate([positions, velocity, rho[None]], axis=0)
    before, after = swap(fields, 1, "chan", True)
    wide = jnp.concatenate([before, fields, after], axis=1)
    below, above = swap(wide, 2, "cross", False)
    ext = jnp.concatenate([below, wide, above], axis=2)
    ext = jnp.pad(ext, ((0, 0), (0, 0), (BASE - HALO, SLOTS - NY - HALO - BASE), (0, 0)))
    new_fields, low = sph_step(ext.reshape(5, NB, S))
    return (new_fields, minimum_everywhere(low))


def solution(mesh):
    return jax.shard_map(
        body,
        mesh=mesh,
        in_specs=(
            P(None, "chan", "cross", None),
            P(None, "chan", "cross", None),
            P("chan", "cross", None),
            P("chan", "cross"),
        ),
        out_specs=(P(None, "chan", "cross", None), P()),
        check_vma=False,
    )
```

```python
import math

import jax
import jax.numpy as jnp
from jax import lax
from jax.experimental import pallas as pl
from jax.experimental.pallas import tpu as pltpu
from jax.sharding import PartitionSpec as P

SOUND_SQ = 100.0
KERNEL_GRAD = 140.0 / math.pi
PARTICLE_MASS = 1.0 / 128.0
GRAVITY = 1.0
TIME_STEP = 0.025
FORCE_SCALE = KERNEL_GRAD * PARTICLE_MASS
HALF = 0.5 * TIME_STEP

S = 128
NX = 4
NY = 16
HALO = 2
COLS = NX + 2 * HALO
SLOTS = NY + 2 * HALO + 4
BASE = HALO + 2
NB = COLS * SLOTS
PLANE_ROWS = NB + 8
SUMF = 24
EXTRA = 8
TALL = 32
OFFSETS = ((0, 0), (0, 1), (1, -1), (1, 0), (1, 1))
DIRECT = (0, 1)
CHAIN = 2
FAR = 1000.0
PLANE = 32


def split(x, pieces):
    out = []
    for _ in range(pieces - 1):
        h = x.astype(jnp.bfloat16).astype(jnp.float32)
        out.append(h)
        x = x - h
    out.append(x)
    return out


def on_grid(x, y):
    row = lax.broadcasted_iota(jnp.int32, (NB, S), 0)
    col = (row * 171) >> 12
    slot = row - col * SLOTS
    return (
        x + (col.astype(jnp.float32) - 0.5 * (COLS - 1)),
        y + (slot.astype(jnp.float32) - 0.5 * (SLOTS - 1)),
    )


def build(x, y, u, v, rho, occ, low, high, refs):
    plane_ref, turned_ref, gx_ref, gy_ref, p_ref, u_ref, v_ref, acc_ref, extra_ref = refs
    acc_ref[...] = jnp.zeros_like(acc_ref)
    extra_ref[...] = jnp.zeros_like(extra_ref)
    gx, gy = on_grid(x, y)
    gx_ref[...] = jnp.where(occ > 0.0, gx, FAR)
    gy_ref[...] = gy
    p = SOUND_SQ * (rho - 1.0) * occ
    p_ref[...] = p
    u_ref[...] = u
    v_ref[...] = v
    gx = gx * occ
    gy = gy * occ
    rows = [occ] + split(gx, 3) + split(gy, 3) + split(u, 2) + split(v, 2) + split(u * gx + v * gy, 3)
    rows += split(p, 2) + split(p * gx, 3) + split(p * gy, 3)
    rows += [jnp.zeros((NB, S), jnp.float32)] * (SUMF - len(rows))
    for f, val in enumerate(rows):
        plane_ref[f * PLANE_ROWS : f * PLANE_ROWS + NB, :] = val

    def turn(r, carry):
        block = plane_ref[pl.ds(r, SUMF, stride=PLANE_ROWS), :]
        block = jnp.concatenate([block, jnp.zeros((TALL - SUMF, S), jnp.float32)], axis=0)
        turned_ref[r] = block.astype(jnp.bfloat16)
        return carry

    lax.fori_loop(low, high, turn, 0, unroll=8)


def geometry(a, bins, refs):
    gx_ref, gy_ref = refs[2], refs[3]
    ax = down(gx_ref, a)
    ay = down(gy_ref, a)
    for b in bins:
        dx = ax - gx_ref[pl.ds(b, 1), :]
        dy = ay - gy_ref[pl.ds(b, 1), :]
        t = jnp.maximum(dx * dx + dy * dy, 1e-30)
        q = jnp.maximum(1.0 - t * lax.rsqrt(t), 0.0)
        yield b, dx, dy, q * q * q


def down(ref, a):
    return jnp.broadcast_to(ref[pl.ds(a, 1), :], (S, S)).T


def column_sums(chain, ks, fine, refs):
    turned_ref = refs[1]
    direct = DIRECT if fine else ()
    p_ref, u_ref, v_ref, acc_ref, extra_ref = refs[4:9]
    out = []
    tiles = []
    for a in chain:
        bins = [a + OFFSETS[k][0] * SLOTS + OFFSETS[k][1] for k in ks]
        rows = []
        mine = {}
        for k, (b, dx, dy, w) in zip(ks, geometry(a, bins, refs)):
            if k not in direct:
                mine[k] = [w.astype(jnp.bfloat16)]
                if fine:
                    mine[k].append((w - mine[k][0].astype(jnp.float32)).astype(jnp.bfloat16))
                continue
            if not rows:
                ap, au, av = (down(ref, a) for ref in (p_ref, u_ref, v_ref))
            at = pl.ds(b, 1)
            wx = w * dx
            wy = w * dy
            p = ap + p_ref[at, :]
            vals = (p * wx, p * wy, (au - u_ref[at, :]) * wx + (av - v_ref[at, :]) * wy)
            rows = [r + x for r, x in zip(rows, vals)] if rows else list(vals)
            if k != 0:
                fx, fy, co = (jnp.sum(x, axis=0, keepdims=True) for x in vals)
                out.append((extra_ref, b * EXTRA, fill_rows(-fx, -fy, co)))
        if rows:
            rows = [jnp.sum(r.T, axis=0, keepdims=True) for r in rows]
            out.append((extra_ref, a * EXTRA, fill_rows(*rows)))
        tiles.append(mine)
        others = [k for k in mine if k != 0]
        to_b = sum(
            jnp.dot(turned_ref[a], jnp.concatenate([mine[k][n] for k in others], axis=1), preferred_element_type=jnp.float32)
            for n in range(2 if fine else 1)
        )
        for n, k in enumerate(others):
            b = a + OFFSETS[k][0] * SLOTS + OFFSETS[k][1]
            out.append((acc_ref, b * SUMF, to_b[:SUMF, n * S : (n + 1) * S]))
    base = chain[0]
    partners = sorted({(OFFSETS[k][0], OFFSETS[k][1] + m) for m, mine in enumerate(tiles) for k in mine})
    right = jnp.concatenate([turned_ref[base + i * SLOTS + j] for i, j in partners], axis=1)
    none = jnp.zeros((S, S), jnp.bfloat16)
    to_a = 0.0
    for n in range(2 if fine else 1):
        w = []
        for m, mine in enumerate(tiles):
            at = {(OFFSETS[k][0], OFFSETS[k][1] + m): mine[k][n] for k in mine}
            w.append(jnp.concatenate([at.get(ij, none) for ij in partners], axis=1))
        w = jnp.concatenate(w, axis=0)
        to_a = to_a + lax.dot_general(right, w, (((1,), (1,)), ((), ())), preferred_element_type=jnp.float32)
    for m, a in enumerate(chain):
        out.append((acc_ref, a * SUMF, to_a[:SUMF, m * S : (m + 1) * S]))
    return out


def fill_rows(*rows):
    return jnp.concatenate([*rows, jnp.zeros((8 - len(rows), S), jnp.float32)], axis=0)


def interact(many, ks, fine, refs):
    sums = [column_sums(chain, ks, fine, refs) for chain in many]
    for group in sums:
        for ref, row, val in group:
            at = pl.ds(pl.multiple_of(row, 8), val.shape[0])
            ref[at, :] = ref[at, :] + val


def sweep(ring, fine, many, refs):
    c0, c1 = ring + 1, COLS - 2 - ring
    s0, s1 = ring + 3, SLOTS - 4 - ring
    wide, tall = c1 - c0 + 1, s1 - s0 + 1
    step = wide // many

    def column(c, carry):
        def row(t, carry):
            a = c * SLOTS + s0 + CHAIN * t
            interact([[a + step * m * SLOTS + n for n in range(CHAIN)] for m in range(many)], (0, 1, 2, 3, 4), fine, refs)
            return carry

        return lax.fori_loop(0, tall // CHAIN, row, carry)

    lax.fori_loop(c0, c0 + step, column, 0)

    def bottom(t, carry):
        interact([[(c0 + 2 * t + m) * SLOTS + s0 - 1] for m in range(2)], (1, 4), fine, refs)
        return carry

    lax.fori_loop(0, wide // 2, bottom, 0)
    n = tall + 2
    total = n + wide - 1
    group = 5 if total % 5 == 0 else 7 if total % 7 == 0 else 1

    def rim(i, carry):
        ts = [i * group + m for m in range(group)]
        at = [jnp.where(t < n, (c0 - 1) * SLOTS + s0 - 1 + t, (c0 + t - n) * SLOTS + s1 + 1) for t in ts]
        interact([[a] for a in at], (2, 3, 4), fine, refs)
        return carry

    lax.fori_loop(0, total // group, rim, 0)


def gather_rates(x, y, u, v, rho, occ, fine, acc_ref, extra_ref):
    def get(f):
        return acc_ref[pl.ds(f, NB, stride=SUMF), :]

    gx, gy = on_grid(x, y)
    s1 = get(0)
    dx = gx * s1 - (get(1) + (get(2) + get(3)))
    dy = gy * s1 - (get(4) + (get(5) + get(6)))
    se = get(11) + (get(12) + get(13))
    comp = u * dx + v * dy - (gx * (get(7) + get(8)) + gy * (get(9) + get(10)) - se)
    p = SOUND_SQ * (rho - 1.0) * occ
    sp = get(14) + get(15)
    fx = p * dx + (gx * sp - (get(16) + (get(17) + get(18))))
    fy = p * dy + (gy * sp - (get(19) + (get(20) + get(21))))
    if fine:
        own = [extra_ref[pl.ds(f, NB, stride=EXTRA), :] for f in range(3)]
        fx = fx + own[0]
        fy = fy + own[1]
        comp = comp + own[2]
    return FORCE_SCALE * fx, FORCE_SCALE * fy - GRAVITY, -FORCE_SCALE * comp


def step_kernel(mid_ref, before_ref, after_ref, below_ref, above_ref, new_ref, low_ref, ext_ref, *refs):
    edge = jnp.zeros((BASE - HALO, S), jnp.float32)
    for f in range(5):
        for c in range(COLS):
            if c < HALO:
                mid = before_ref[f, c]
            elif c < HALO + NX:
                mid = mid_ref[f, c - HALO]
            else:
                mid = after_ref[f, c - HALO - NX]
            rows = [edge, below_ref[f, c], mid, above_ref[f, c], edge]
            ext_ref[f, c * SLOTS : (c + 1) * SLOTS, :] = jnp.concatenate(rows, axis=0)

    def load():
        rho = ext_ref[4]
        occ = jnp.where(rho > 0.0, 1.0, 0.0)
        x = (ext_ref[0] - 0.5) * occ
        y = (ext_ref[1] - 0.5) * occ
        return x, y, ext_ref[2] * occ, ext_ref[3] * occ, rho, occ

    x, y, u, v, rho, occ = load()
    build(x, y, u, v, rho, occ, 0, NB, refs)
    sweep(0, False, 6, refs)
    x, y, u, v, rho, occ = load()
    ax, ay, ar = gather_rates(x, y, u, v, rho, occ, False, *refs[-2:])

    def predicted():
        return (
            (x + HALF * u) * occ,
            (y + HALF * v) * occ,
            (u + HALF * ax) * occ,
            (v + HALF * ay) * occ,
            (rho + HALF * ar) * occ,
        )

    px, py, pu, pv, pr = predicted()
    build(px, py, pu, pv, pr, occ, SLOTS, NB - SLOTS, refs)
    sweep(1, True, 4, refs)
    ax, ay, ar = gather_rates(px, py, pu, pv, pr, occ, True, *refs[-2:])
    x, y, u, v, rho, occ = load()
    nu = u + TIME_STEP * ax
    nv = v + TIME_STEP * ay
    nx = ext_ref[0] + HALF * (u + nu)
    ny = ext_ref[1] + HALF * (v + nv)
    nr = rho + TIME_STEP * ar
    low = jnp.where(occ > 0.0, nr, 1000000000.0)
    lows = []
    for c in range(NX):
        at = slice((c + HALO) * SLOTS + BASE, (c + HALO) * SLOTS + BASE + NY)
        for f, val in enumerate((nx, ny, nu, nv, nr)):
            new_ref[f, c] = jnp.where(occ[at] > 0.0, val[at], 0.0)
        lows.append(low[at])
    low_ref[...] = jnp.broadcast_to(jnp.min(jnp.concatenate(lows, axis=0)), low_ref.shape)


def sph_step(*pieces):
    return pl.pallas_call(
        step_kernel,
        out_shape=(
            jax.ShapeDtypeStruct((5, NX, NY, S), jnp.float32),
            jax.ShapeDtypeStruct((PLANE, S), jnp.float32),
        ),
        in_specs=[pl.BlockSpec(memory_space=pltpu.VMEM)] * 5,
        out_specs=(
            pl.BlockSpec(memory_space=pltpu.VMEM),
            pl.BlockSpec(memory_space=pltpu.VMEM),
        ),
        scratch_shapes=[
            pltpu.VMEM((5, NB, S), jnp.float32),
            pltpu.VMEM((SUMF * PLANE_ROWS, S), jnp.float32),
            pltpu.VMEM((NB, TALL, S), jnp.bfloat16),
            pltpu.VMEM((NB, S), jnp.float32),
            pltpu.VMEM((NB, S), jnp.float32),
            pltpu.VMEM((NB, S), jnp.float32),
            pltpu.VMEM((NB, S), jnp.float32),
            pltpu.VMEM((NB, S), jnp.float32),
            pltpu.VMEM((NB * SUMF, S), jnp.float32),
            pltpu.VMEM((NB * EXTRA, S), jnp.float32),
        ],
        name="sph_step",
    )(*pieces)


def swap(x, dim, axis, wrap):
    size, length = lax.axis_size(axis), x.shape[dim]
    even = lax.axis_index(axis) % 2 == 0
    last = lax.slice_in_dim(x, length - HALO, length, axis=dim)
    first = lax.slice_in_dim(x, 0, HALO, axis=dim)

    def pairs(start):
        ends = [(i, (i + 1) % size) for i in range(start, size if wrap else size - 1, 2)]
        return ends + [(j, i) for i, j in ends]

    near = lax.ppermute(jnp.where(even, last, first), axis, pairs(0))
    far = lax.ppermute(jnp.where(even, first, last), axis, pairs(1))
    return jnp.where(even, far, near), jnp.where(even, near, far)


def minimum_everywhere(low):
    chan, cross = lax.axis_size("chan"), lax.axis_size("cross")
    planes = {}
    for i in range(chan * cross):
        planes.setdefault((i // cross // 4 % 8, i % cross // 2), []).append(i)
    planes = list(planes.values())
    lines = [list(line) for line in zip(*planes)]
    both = ("chan", "cross")
    got = lax.all_to_all(low, both, 0, 0, tiled=True, axis_index_groups=planes)
    got = jnp.broadcast_to(jnp.min(got, axis=0, keepdims=True), (len(planes), S))
    return jnp.min(lax.all_to_all(got, both, 0, 0, tiled=True, axis_index_groups=lines))


def body(positions, velocity, density, counts):
    slot_index = jnp.arange(S, dtype=jnp.int32)
    rho = jnp.where(slot_index[None, None, :] < counts[:, :, None], density, 0.0)
    fields = jnp.concatenate([positions, velocity, rho[None]], axis=0)
    before, after = swap(fields, 1, "chan", True)
    wide = jnp.concatenate([before, fields, after], axis=1)
    below, above = swap(wide, 2, "cross", False)
    new_fields, low = sph_step(fields, before, after, below, above)
    return (new_fields, minimum_everywhere(low))


def solution(mesh):
    return jax.shard_map(
        body,
        mesh=mesh,
        in_specs=(
            P(None, "chan", "cross", None),
            P(None, "chan", "cross", None),
            P("chan", "cross", None),
            P("chan", "cross"),
        ),
        out_specs=(P(None, "chan", "cross", None), P()),
        check_vma=False,
    )
```

```python
import math

import jax
import jax.numpy as jnp
from jax import lax
from jax.experimental import pallas as pl
from jax.experimental.pallas import tpu as pltpu
from jax.sharding import PartitionSpec as P

SOUND_SQ = 100.0
KERNEL_GRAD = 140.0 / math.pi
PARTICLE_MASS = 1.0 / 128.0
GRAVITY = 1.0
TIME_STEP = 0.025
FORCE_SCALE = KERNEL_GRAD * PARTICLE_MASS
HALF = 0.5 * TIME_STEP

S = 128
NX = 4
NY = 16
HALO = 2
COLS = NX + 2 * HALO
SLOTS = NY + 2 * HALO + 4
BASE = HALO + 2
NB = COLS * SLOTS
PLANE_ROWS = NB + 8
SUMF = 24
EXTRA = 8
TALL = 32
OFFSETS = ((0, 0), (0, 1), (1, -1), (1, 0), (1, 1))
DIRECT = (0, 1)
CHAIN = 2
OWN = HALO * SLOTS
FAR = 1000.0
PLANE = 32


def split(x, pieces):
    out = []
    for _ in range(pieces - 1):
        h = x.astype(jnp.bfloat16).astype(jnp.float32)
        out.append(h)
        x = x - h
    out.append(x)
    return out


def on_grid(x, y, first=0):
    row = first + lax.broadcasted_iota(jnp.int32, x.shape, 0)
    col = (row * 171) >> 12
    slot = row - col * SLOTS
    return (
        x + (col.astype(jnp.float32) - 0.5 * (COLS - 1)),
        y + (slot.astype(jnp.float32) - 0.5 * (SLOTS - 1)),
    )


def build(x, y, u, v, rho, occ, first, low, high, refs):
    plane_ref, turned_ref, gx_ref, gy_ref, p_ref, u_ref, v_ref, acc_ref, extra_ref = refs
    acc_ref[...] = jnp.zeros_like(acc_ref)
    extra_ref[...] = jnp.zeros_like(extra_ref)
    gx, gy = on_grid(x, y, first)
    n = x.shape[0]
    at = slice(first, first + n)
    gx_ref[at] = jnp.where(occ > 0.0, gx, FAR)
    gy_ref[at] = gy
    p = SOUND_SQ * (rho - 1.0) * occ
    p_ref[at] = p
    u_ref[at] = u
    v_ref[at] = v
    gx = gx * occ
    gy = gy * occ
    rows = [occ] + split(gx, 3) + split(gy, 3) + split(u, 2) + split(v, 2) + split(u * gx + v * gy, 3)
    rows += split(p, 2) + split(p * gx, 3) + split(p * gy, 3)
    rows += [jnp.zeros((n, S), jnp.float32)] * (SUMF - len(rows))
    for f, val in enumerate(rows):
        plane_ref[f * PLANE_ROWS + first : f * PLANE_ROWS + first + n, :] = val

    def turn(r, carry):
        block = plane_ref[pl.ds(r, SUMF, stride=PLANE_ROWS), :]
        block = jnp.concatenate([block, jnp.zeros((TALL - SUMF, S), jnp.float32)], axis=0)
        turned_ref[r] = block.astype(jnp.bfloat16)
        return carry

    lax.fori_loop(low, high, turn, 0, unroll=8)


def geometry(a, bins, refs):
    gx_ref, gy_ref = refs[2], refs[3]
    ax = down(gx_ref, a)
    ay = down(gy_ref, a)
    for b in bins:
        dx = ax - gx_ref[pl.ds(b, 1), :]
        dy = ay - gy_ref[pl.ds(b, 1), :]
        t = dx * dx + dy * dy
        q = jnp.maximum(1.0 - t * lax.rsqrt(jnp.maximum(t, 1e-30)), 0.0)
        yield b, dx, dy, q * q * q


def down(ref, a):
    return jnp.broadcast_to(ref[pl.ds(a, 1), :], (S, S)).T


def column_sums(chain, ks, fine, refs):
    turned_ref = refs[1]
    direct = DIRECT if fine else ()
    p_ref, u_ref, v_ref, acc_ref, extra_ref = refs[4:9]
    out = []
    tiles = []
    for a in chain:
        bins = [a + OFFSETS[k][0] * SLOTS + OFFSETS[k][1] for k in ks]
        rows = []
        mine = {}
        for k, (b, dx, dy, w) in zip(ks, geometry(a, bins, refs)):
            if k not in direct:
                mine[k] = [w.astype(jnp.bfloat16)]
                if fine:
                    mine[k].append((w - mine[k][0].astype(jnp.float32)).astype(jnp.bfloat16))
                continue
            if not rows:
                ap, au, av = (down(ref, a) for ref in (p_ref, u_ref, v_ref))
            at = pl.ds(b, 1)
            wx = w * dx
            wy = w * dy
            p = ap + p_ref[at, :]
            vals = (p * wx, p * wy, (au - u_ref[at, :]) * wx + (av - v_ref[at, :]) * wy)
            rows = [r + x for r, x in zip(rows, vals)] if rows else list(vals)
            if k != 0:
                fx, fy, co = (jnp.sum(x, axis=0, keepdims=True) for x in vals)
                out.append((extra_ref, b * EXTRA, fill_rows(-fx, -fy, co)))
        if rows:
            rows = [jnp.sum(r.T, axis=0, keepdims=True) for r in rows]
            out.append((extra_ref, a * EXTRA, fill_rows(*rows)))
        tiles.append(mine)
        others = [k for k in mine if k != 0]
        to_b = sum(
            jnp.dot(turned_ref[a], jnp.concatenate([mine[k][n] for k in others], axis=1), preferred_element_type=jnp.float32)
            for n in range(2 if fine else 1)
        )
        for n, k in enumerate(others):
            b = a + OFFSETS[k][0] * SLOTS + OFFSETS[k][1]
            out.append((acc_ref, b * SUMF, to_b[:SUMF, n * S : (n + 1) * S]))
    base = chain[0]
    partners = sorted({(OFFSETS[k][0], OFFSETS[k][1] + m) for m, mine in enumerate(tiles) for k in mine})
    right = jnp.concatenate([turned_ref[base + i * SLOTS + j] for i, j in partners], axis=1)
    none = jnp.zeros((S, S), jnp.bfloat16)
    to_a = 0.0
    for n in range(2 if fine else 1):
        w = []
        for m, mine in enumerate(tiles):
            at = {(OFFSETS[k][0], OFFSETS[k][1] + m): mine[k][n] for k in mine}
            w.append(jnp.concatenate([at.get(ij, none) for ij in partners], axis=1))
        w = jnp.concatenate(w, axis=0)
        to_a = to_a + lax.dot_general(right, w, (((1,), (1,)), ((), ())), preferred_element_type=jnp.float32)
    for m, a in enumerate(chain):
        out.append((acc_ref, a * SUMF, to_a[:SUMF, m * S : (m + 1) * S]))
    return out


def fill_rows(*rows):
    return jnp.concatenate([*rows, jnp.zeros((8 - len(rows), S), jnp.float32)], axis=0)


def interact(many, ks, fine, refs):
    sums = [column_sums(chain, ks, fine, refs) for chain in many]
    for group in sums:
        for ref, row, val in group:
            at = pl.ds(pl.multiple_of(row, 8), val.shape[0])
            ref[at, :] = ref[at, :] + val


def chains(bins):
    return [[a + n for n in range(CHAIN)] for a in bins]


ALL = (0, 1, 2, 3, 4)
NEXT = (2, 3, 4)
SAME = (0, 1)
LOW, TOP = BASE + 1, BASE + NY - CHAIN


def sweep_inner(refs):
    def row(t, carry):
        s = LOW + CHAIN * t
        interact(chains([c * SLOTS + s for c in range(HALO, HALO + NX - 1)]), ALL, False, refs)
        interact(chains([(HALO + NX - 1) * SLOTS + s]), SAME, False, refs)
        return carry

    lax.fori_loop(0, (NY - 2) // CHAIN, row, 0)


def sweep_outer(refs):
    last = HALO + NX

    def side(t, carry):
        s = LOW - CHAIN + 3 * CHAIN * t
        bins = [c * SLOTS + s + CHAIN * m for m in range(3) for c in (HALO - 1, last)]
        interact(chains(bins), ALL, False, refs)
        return carry

    lax.fori_loop(0, (NY + 2) // (3 * CHAIN), side, 0)

    def end(t, carry):
        s = LOW - CHAIN + t * (NY)
        interact(chains([c * SLOTS + s for c in range(HALO, last)]), ALL, False, refs)
        return carry

    lax.fori_loop(0, 2, end, 0)
    interact(chains([(last - 1) * SLOTS + LOW + CHAIN * m for m in range((NY - 2) // CHAIN)]), NEXT, False, refs)


def sweep_all(ring, fine, many, refs):
    c0, c1 = ring + 1, COLS - 2 - ring
    s0, s1 = ring + 3, SLOTS - 4 - ring
    wide, tall = c1 - c0 + 1, s1 - s0 + 1
    step = wide // many

    def column(c, carry):
        def row(t, carry):
            a = c * SLOTS + s0 + CHAIN * t
            interact(chains([a + step * m * SLOTS for m in range(many)]), ALL, fine, refs)
            return carry

        return lax.fori_loop(0, tall // CHAIN, row, carry)

    lax.fori_loop(c0, c0 + step, column, 0)


def sweep_rim(ring, fine, refs):
    c0, c1 = ring + 1, COLS - 2 - ring
    s0, s1 = ring + 3, SLOTS - 4 - ring
    wide, tall = c1 - c0 + 1, s1 - s0 + 1

    def bottom(t, carry):
        interact([[(c0 + 2 * t + m) * SLOTS + s0 - 1] for m in range(2)], (1, 4), fine, refs)
        return carry

    lax.fori_loop(0, wide // 2, bottom, 0)
    n = tall + 2
    total = n + wide - 1
    group = 5 if total % 5 == 0 else 7 if total % 7 == 0 else 1

    def rim(i, carry):
        ts = [i * group + m for m in range(group)]
        at = [jnp.where(t < n, (c0 - 1) * SLOTS + s0 - 1 + t, (c0 + t - n) * SLOTS + s1 + 1) for t in ts]
        interact([[a] for a in at], NEXT, fine, refs)
        return carry

    lax.fori_loop(0, total // group, rim, 0)


def gather_rates(x, y, u, v, rho, occ, fine, acc_ref, extra_ref):
    def get(f):
        return acc_ref[pl.ds(f, NB, stride=SUMF), :]

    gx, gy = on_grid(x, y)
    s1 = get(0)
    dx = gx * s1 - (get(1) + (get(2) + get(3)))
    dy = gy * s1 - (get(4) + (get(5) + get(6)))
    se = get(11) + (get(12) + get(13))
    comp = u * dx + v * dy - (gx * (get(7) + get(8)) + gy * (get(9) + get(10)) - se)
    p = SOUND_SQ * (rho - 1.0) * occ
    sp = get(14) + get(15)
    fx = p * dx + (gx * sp - (get(16) + (get(17) + get(18))))
    fy = p * dy + (gy * sp - (get(19) + (get(20) + get(21))))
    if fine:
        own = [extra_ref[pl.ds(f, NB, stride=EXTRA), :] for f in range(3)]
        fx = fx + own[0]
        fy = fy + own[1]
        comp = comp + own[2]
    return FORCE_SCALE * fx, FORCE_SCALE * fy - GRAVITY, -FORCE_SCALE * comp


def step_kernel(mid_ref, before_ref, after_ref, below_ref, above_ref, inner_ref, new_ref, low_ref, ext_ref, *refs):
    acc_ref = refs[-2]
    edge = jnp.zeros((BASE - HALO, S), jnp.float32)
    for f in range(5):
        for c in range(COLS):
            if c < HALO:
                mid = before_ref[f, c]
            elif c < HALO + NX:
                mid = mid_ref[f, c - HALO]
            else:
                mid = after_ref[f, c - HALO - NX]
            rows = [edge, below_ref[f, c], mid, above_ref[f, c], edge]
            ext_ref[f, c * SLOTS : (c + 1) * SLOTS, :] = jnp.concatenate(rows, axis=0)

    def load():
        rho = ext_ref[4]
        occ = jnp.where(rho > 0.0, 1.0, 0.0)
        x = (ext_ref[0] - 0.5) * occ
        y = (ext_ref[1] - 0.5) * occ
        return x, y, ext_ref[2] * occ, ext_ref[3] * occ, rho, occ

    x, y, u, v, rho, occ = load()
    build(x, y, u, v, rho, occ, 0, 0, NB, refs)
    acc_ref[OWN * SUMF : (OWN + NX * SLOTS) * SUMF, :] = inner_ref[...]
    sweep_outer(refs)
    sweep_rim(0, False, refs)
    x, y, u, v, rho, occ = load()
    ax, ay, ar = gather_rates(x, y, u, v, rho, occ, False, *refs[-2:])

    def predicted():
        return (
            (x + HALF * u) * occ,
            (y + HALF * v) * occ,
            (u + HALF * ax) * occ,
            (v + HALF * ay) * occ,
            (rho + HALF * ar) * occ,
        )

    px, py, pu, pv, pr = predicted()
    build(px, py, pu, pv, pr, occ, 0, SLOTS, NB - SLOTS, refs)
    sweep_all(1, True, 4, refs)
    sweep_rim(1, True, refs)
    ax, ay, ar = gather_rates(px, py, pu, pv, pr, occ, True, *refs[-2:])
    x, y, u, v, rho, occ = load()
    nu = u + TIME_STEP * ax
    nv = v + TIME_STEP * ay
    nx = ext_ref[0] + HALF * (u + nu)
    ny = ext_ref[1] + HALF * (v + nv)
    nr = rho + TIME_STEP * ar
    low = jnp.where(occ > 0.0, nr, 1000000000.0)
    lows = []
    for c in range(NX):
        at = slice((c + HALO) * SLOTS + BASE, (c + HALO) * SLOTS + BASE + NY)
        for f, val in enumerate((nx, ny, nu, nv, nr)):
            new_ref[f, c] = jnp.where(occ[at] > 0.0, val[at], 0.0)
        lows.append(low[at])
    low_ref[...] = jnp.broadcast_to(jnp.min(jnp.concatenate(lows, axis=0)), low_ref.shape)


def scratch():
    return [
        pltpu.VMEM((SUMF * PLANE_ROWS, S), jnp.float32),
        pltpu.VMEM((NB, TALL, S), jnp.bfloat16),
        *[pltpu.VMEM((NB, S), jnp.float32) for _ in range(5)],
        pltpu.VMEM((NB * SUMF, S), jnp.float32),
        pltpu.VMEM((NB * EXTRA, S), jnp.float32),
    ]


def inner_kernel(mid_ref, inner_ref, *refs):
    edge = jnp.zeros((BASE, S), jnp.float32)

    def grid(f):
        return jnp.concatenate([rows for c in range(NX) for rows in (edge, mid_ref[f, c], edge)], axis=0)

    rho = grid(4)
    occ = jnp.where(rho > 0.0, 1.0, 0.0)
    x = (grid(0) - 0.5) * occ
    y = (grid(1) - 0.5) * occ
    build(x, y, grid(2) * occ, grid(3) * occ, rho, occ, OWN, OWN, OWN + NX * SLOTS, refs)
    sweep_inner(refs)
    inner_ref[...] = refs[-2][OWN * SUMF : (OWN + NX * SLOTS) * SUMF, :]


def sph_inner(mid):
    return pl.pallas_call(
        inner_kernel,
        out_shape=jax.ShapeDtypeStruct((NX * SLOTS * SUMF, S), jnp.float32),
        in_specs=[pl.BlockSpec(memory_space=pltpu.VMEM)],
        out_specs=pl.BlockSpec(memory_space=pltpu.VMEM),
        scratch_shapes=scratch(),
        cost_estimate=pl.CostEstimate(flops=8000000000, transcendentals=0, bytes_accessed=1000000),
        name="sph_inner",
    )(mid)


def sph_step(*pieces):
    return pl.pallas_call(
        step_kernel,
        out_shape=(
            jax.ShapeDtypeStruct((5, NX, NY, S), jnp.float32),
            jax.ShapeDtypeStruct((PLANE, S), jnp.float32),
        ),
        in_specs=[pl.BlockSpec(memory_space=pltpu.VMEM)] * 6,
        out_specs=(
            pl.BlockSpec(memory_space=pltpu.VMEM),
            pl.BlockSpec(memory_space=pltpu.VMEM),
        ),
        scratch_shapes=[pltpu.VMEM((5, NB, S), jnp.float32), *scratch()],
        name="sph_step",
    )(*pieces)


def swap(x, dim, axis, wrap):
    size, length = lax.axis_size(axis), x.shape[dim]
    even = lax.axis_index(axis) % 2 == 0
    last = lax.slice_in_dim(x, length - HALO, length, axis=dim)
    first = lax.slice_in_dim(x, 0, HALO, axis=dim)

    def pairs(start):
        ends = [(i, (i + 1) % size) for i in range(start, size if wrap else size - 1, 2)]
        return ends + [(j, i) for i, j in ends]

    near = lax.ppermute(jnp.where(even, last, first), axis, pairs(0))
    far = lax.ppermute(jnp.where(even, first, last), axis, pairs(1))
    return jnp.where(even, far, near), jnp.where(even, near, far)


def minimum_everywhere(low):
    chan, cross = lax.axis_size("chan"), lax.axis_size("cross")
    planes = {}
    for i in range(chan * cross):
        planes.setdefault((i // cross // 4 % 8, i % cross // 2), []).append(i)
    planes = list(planes.values())
    lines = [list(line) for line in zip(*planes)]
    both = ("chan", "cross")
    got = lax.all_to_all(low, both, 0, 0, tiled=True, axis_index_groups=planes)
    got = jnp.broadcast_to(jnp.min(got, axis=0, keepdims=True), (len(planes), S))
    return jnp.min(lax.all_to_all(got, both, 0, 0, tiled=True, axis_index_groups=lines))


def body(positions, velocity, density, counts):
    slot_index = jnp.arange(S, dtype=jnp.int32)
    rho = jnp.where(slot_index[None, None, :] < counts[:, :, None], density, 0.0)
    fields = jnp.concatenate([positions, velocity, rho[None]], axis=0)
    before, after = swap(fields, 1, "chan", True)
    wide = jnp.concatenate([before, fields, after], axis=1)
    below, above = swap(wide, 2, "cross", False)
    new_fields, low = sph_step(fields, before, after, below, above, sph_inner(fields))
    return (new_fields, minimum_everywhere(low))


def solution(mesh):
    return jax.shard_map(
        body,
        mesh=mesh,
        in_specs=(
            P(None, "chan", "cross", None),
            P(None, "chan", "cross", None),
            P("chan", "cross", None),
            P("chan", "cross"),
        ),
        out_specs=(P(None, "chan", "cross", None), P()),
        check_vma=False,
    )
```

```python
import math

import jax
import jax.numpy as jnp
from jax import lax
from jax.experimental import pallas as pl
from jax.experimental.pallas import tpu as pltpu
from jax.sharding import PartitionSpec as P

SOUND_SQ = 100.0
KERNEL_GRAD = 140.0 / math.pi
PARTICLE_MASS = 1.0 / 128.0
GRAVITY = 1.0
TIME_STEP = 0.025
FORCE_SCALE = KERNEL_GRAD * PARTICLE_MASS
HALF = 0.5 * TIME_STEP

S = 128
NX = 4
NY = 16
HALO = 2
COLS = NX + 2 * HALO
SLOTS = NY + 2 * HALO + 4
BASE = HALO + 2
NB = COLS * SLOTS
PLANE_ROWS = NB + 8
SUMF = 24
EXTRA = 8
TALL = 32
OFFSETS = ((0, 0), (0, 1), (1, -1), (1, 0), (1, 1))
DIRECT = (0, 1)
CHAIN = 2
OWN = HALO * SLOTS
FAR = 1000.0
PLANE = 32


def split(x, pieces):
    out = []
    for _ in range(pieces - 1):
        h = x.astype(jnp.bfloat16).astype(jnp.float32)
        out.append(h)
        x = x - h
    out.append(x)
    return out


def on_grid(x, y, first=0):
    row = first + lax.broadcasted_iota(jnp.int32, x.shape, 0)
    col = (row * 171) >> 12
    slot = row - col * SLOTS
    return (
        x + (col.astype(jnp.float32) - 0.5 * (COLS - 1)),
        y + (slot.astype(jnp.float32) - 0.5 * (SLOTS - 1)),
    )


def build(x, y, u, v, rho, occ, first, low, high, refs):
    plane_ref, turned_ref, gx_ref, gy_ref, p_ref, u_ref, v_ref, acc_ref, extra_ref = refs
    acc_ref[...] = jnp.zeros_like(acc_ref)
    extra_ref[...] = jnp.zeros_like(extra_ref)
    gx, gy = on_grid(x, y, first)
    n = x.shape[0]
    at = slice(first, first + n)
    gx_ref[at] = jnp.where(occ > 0.0, gx, FAR)
    gy_ref[at] = gy
    p = SOUND_SQ * (rho - 1.0) * occ
    p_ref[at] = p
    u_ref[at] = u
    v_ref[at] = v
    gx = gx * occ
    gy = gy * occ
    rows = [occ] + split(gx, 3) + split(gy, 3) + split(u, 2) + split(v, 2) + split(u * gx + v * gy, 3)
    rows += split(p, 2) + split(p * gx, 3) + split(p * gy, 3)
    rows += [jnp.zeros((n, S), jnp.float32)] * (SUMF - len(rows))
    for f, val in enumerate(rows):
        plane_ref[f * PLANE_ROWS + first : f * PLANE_ROWS + first + n, :] = val

    def turn(r, carry):
        block = plane_ref[pl.ds(r, SUMF, stride=PLANE_ROWS), :]
        block = jnp.concatenate([block, jnp.zeros((TALL - SUMF, S), jnp.float32)], axis=0)
        turned_ref[r] = block.astype(jnp.bfloat16)
        return carry

    lax.fori_loop(low, high, turn, 0, unroll=8)


def geometry(a, bins, refs):
    gx_ref, gy_ref = refs[2], refs[3]
    ax = down(gx_ref, a)
    ay = down(gy_ref, a)
    for b in bins:
        dx = ax - gx_ref[pl.ds(b, 1), :]
        dy = ay - gy_ref[pl.ds(b, 1), :]
        t = dx * dx + dy * dy
        q = jnp.maximum(1.0 - t * lax.rsqrt(jnp.maximum(t, 1e-30)), 0.0)
        yield b, dx, dy, q * q * q


def down(ref, a):
    return jnp.broadcast_to(ref[pl.ds(a, 1), :], (S, S)).T


def column_sums(chain, ks, fine, refs):
    turned_ref = refs[1]
    direct = DIRECT if fine else ()
    p_ref, u_ref, v_ref, acc_ref, extra_ref = refs[4:9]
    out = []
    tiles = []
    for a in chain:
        bins = [a + OFFSETS[k][0] * SLOTS + OFFSETS[k][1] for k in ks]
        rows = []
        mine = {}
        for k, (b, dx, dy, w) in zip(ks, geometry(a, bins, refs)):
            if k not in direct:
                mine[k] = [w.astype(jnp.bfloat16)]
                if fine:
                    mine[k].append((w - mine[k][0].astype(jnp.float32)).astype(jnp.bfloat16))
                continue
            if not rows:
                ap, au, av = (down(ref, a) for ref in (p_ref, u_ref, v_ref))
            at = pl.ds(b, 1)
            wx = w * dx
            wy = w * dy
            p = ap + p_ref[at, :]
            vals = (p * wx, p * wy, (au - u_ref[at, :]) * wx + (av - v_ref[at, :]) * wy)
            rows = [r + x for r, x in zip(rows, vals)] if rows else list(vals)
            if k != 0:
                fx, fy, co = (jnp.sum(x, axis=0, keepdims=True) for x in vals)
                out.append((extra_ref, b * EXTRA, fill_rows(-fx, -fy, co)))
        if rows:
            rows = [jnp.sum(r.T, axis=0, keepdims=True) for r in rows]
            out.append((extra_ref, a * EXTRA, fill_rows(*rows)))
        tiles.append(mine)
        others = [k for k in mine if k != 0]
        to_b = sum(
            jnp.dot(turned_ref[a], jnp.concatenate([mine[k][n] for k in others], axis=1), preferred_element_type=jnp.float32)
            for n in range(2 if fine else 1)
        )
        for n, k in enumerate(others):
            b = a + OFFSETS[k][0] * SLOTS + OFFSETS[k][1]
            out.append((acc_ref, b * SUMF, to_b[:SUMF, n * S : (n + 1) * S]))
    base = chain[0]
    partners = sorted({(OFFSETS[k][0], OFFSETS[k][1] + m) for m, mine in enumerate(tiles) for k in mine})
    right = jnp.concatenate([turned_ref[base + i * SLOTS + j] for i, j in partners], axis=1)
    none = jnp.zeros((S, S), jnp.bfloat16)
    to_a = 0.0
    for n in range(2 if fine else 1):
        w = []
        for m, mine in enumerate(tiles):
            at = {(OFFSETS[k][0], OFFSETS[k][1] + m): mine[k][n] for k in mine}
            w.append(jnp.concatenate([at.get(ij, none) for ij in partners], axis=1))
        w = jnp.concatenate(w, axis=0)
        to_a = to_a + lax.dot_general(right, w, (((1,), (1,)), ((), ())), preferred_element_type=jnp.float32)
    for m, a in enumerate(chain):
        out.append((acc_ref, a * SUMF, to_a[:SUMF, m * S : (m + 1) * S]))
    return out


def fill_rows(*rows):
    return jnp.concatenate([*rows, jnp.zeros((8 - len(rows), S), jnp.float32)], axis=0)


def interact(many, ks, fine, refs):
    sums = [column_sums(chain, ks, fine, refs) for chain in many]
    for group in sums:
        for ref, row, val in group:
            at = pl.ds(pl.multiple_of(row, 8), val.shape[0])
            ref[at, :] = ref[at, :] + val


def chains(bins):
    return [[a + n for n in range(CHAIN)] for a in bins]


ALL = (0, 1, 2, 3, 4)
NEXT = (2, 3, 4)
SAME = (0, 1)
LOW = BASE + 1


def sweep_inner(refs):
    def row(t, carry):
        s = LOW + CHAIN * t
        interact(chains([c * SLOTS + s for c in range(HALO, HALO + NX - 1)]), ALL, False, refs)
        interact(chains([(HALO + NX - 1) * SLOTS + s]), SAME, False, refs)
        return carry

    lax.fori_loop(0, (NY - 2) // CHAIN, row, 0)


def sweep_outer(refs):
    last = HALO + NX

    def side(t, carry):
        s = LOW - CHAIN + 3 * CHAIN * t
        bins = [c * SLOTS + s + CHAIN * m for m in range(3) for c in (HALO - 1, last)]
        interact(chains(bins), ALL, False, refs)
        return carry

    lax.fori_loop(0, (NY + 2) // (3 * CHAIN), side, 0)

    def end(t, carry):
        s = LOW - CHAIN + t * (NY)
        interact(chains([c * SLOTS + s for c in range(HALO, last)]), ALL, False, refs)
        return carry

    lax.fori_loop(0, 2, end, 0)
    interact(chains([(last - 1) * SLOTS + LOW + CHAIN * m for m in range((NY - 2) // CHAIN)]), NEXT, False, refs)


def sweep_all(ring, fine, many, refs):
    c0, c1 = ring + 1, COLS - 2 - ring
    s0, s1 = ring + 3, SLOTS - 4 - ring
    wide, tall = c1 - c0 + 1, s1 - s0 + 1
    step = wide // many

    def column(c, carry):
        def row(t, carry):
            a = c * SLOTS + s0 + CHAIN * t
            interact(chains([a + step * m * SLOTS for m in range(many)]), ALL, fine, refs)
            return carry

        return lax.fori_loop(0, tall // CHAIN, row, carry)

    lax.fori_loop(c0, c0 + step, column, 0)


def sweep_rim(ring, fine, refs):
    c0, c1 = ring + 1, COLS - 2 - ring
    s0, s1 = ring + 3, SLOTS - 4 - ring
    wide, tall = c1 - c0 + 1, s1 - s0 + 1

    def bottom(t, carry):
        interact([[(c0 + 2 * t + m) * SLOTS + s0 - 1] for m in range(2)], (1, 4), fine, refs)
        return carry

    lax.fori_loop(0, wide // 2, bottom, 0)
    n = tall + 2
    total = n + wide - 1
    group = 5 if total % 5 == 0 else 7 if total % 7 == 0 else 1

    def rim(i, carry):
        ts = [i * group + m for m in range(group)]
        at = [jnp.where(t < n, (c0 - 1) * SLOTS + s0 - 1 + t, (c0 + t - n) * SLOTS + s1 + 1) for t in ts]
        interact([[a] for a in at], NEXT, fine, refs)
        return carry

    lax.fori_loop(0, total // group, rim, 0)


def gather_rates(x, y, u, v, rho, occ, fine, acc_ref, extra_ref):
    def get(f):
        return acc_ref[pl.ds(f, NB, stride=SUMF), :]

    gx, gy = on_grid(x, y)
    s1 = get(0)
    dx = gx * s1 - (get(1) + (get(2) + get(3)))
    dy = gy * s1 - (get(4) + (get(5) + get(6)))
    se = get(11) + (get(12) + get(13))
    comp = u * dx + v * dy - (gx * (get(7) + get(8)) + gy * (get(9) + get(10)) - se)
    p = SOUND_SQ * (rho - 1.0) * occ
    sp = get(14) + get(15)
    fx = p * dx + (gx * sp - (get(16) + (get(17) + get(18))))
    fy = p * dy + (gy * sp - (get(19) + (get(20) + get(21))))
    if fine:
        own = [extra_ref[pl.ds(f, NB, stride=EXTRA), :] for f in range(3)]
        fx = fx + own[0]
        fy = fy + own[1]
        comp = comp + own[2]
    return FORCE_SCALE * fx, FORCE_SCALE * fy - GRAVITY, -FORCE_SCALE * comp


def step_kernel(mid_ref, before_ref, after_ref, below_ref, above_ref, inner_ref, new_ref, low_ref, ext_ref, *refs):
    acc_ref = refs[-2]
    edge = jnp.zeros((BASE - HALO, S), jnp.float32)
    for f in range(5):
        for c in range(COLS):
            if c < HALO:
                mid = before_ref[f, c]
            elif c < HALO + NX:
                mid = mid_ref[f, c - HALO]
            else:
                mid = after_ref[f, c - HALO - NX]
            rows = [edge, below_ref[f, c], mid, above_ref[f, c], edge]
            ext_ref[f, c * SLOTS : (c + 1) * SLOTS, :] = jnp.concatenate(rows, axis=0)

    def load():
        rho = ext_ref[4]
        occ = jnp.where(rho > 0.0, 1.0, 0.0)
        x = (ext_ref[0] - 0.5) * occ
        y = (ext_ref[1] - 0.5) * occ
        return x, y, ext_ref[2] * occ, ext_ref[3] * occ, rho, occ

    x, y, u, v, rho, occ = load()
    build(x, y, u, v, rho, occ, 0, 0, NB, refs)
    acc_ref[OWN * SUMF : (OWN + NX * SLOTS) * SUMF, :] = inner_ref[...]
    sweep_outer(refs)
    sweep_rim(0, False, refs)
    x, y, u, v, rho, occ = load()
    ax, ay, ar = gather_rates(x, y, u, v, rho, occ, False, *refs[-2:])

    def predicted():
        return (
            (x + HALF * u) * occ,
            (y + HALF * v) * occ,
            (u + HALF * ax) * occ,
            (v + HALF * ay) * occ,
            (rho + HALF * ar) * occ,
        )

    px, py, pu, pv, pr = predicted()
    build(px, py, pu, pv, pr, occ, 0, SLOTS, NB - SLOTS, refs)
    sweep_all(1, True, 4, refs)
    sweep_rim(1, True, refs)
    ax, ay, ar = gather_rates(px, py, pu, pv, pr, occ, True, *refs[-2:])
    x, y, u, v, rho, occ = load()
    nu = u + TIME_STEP * ax
    nv = v + TIME_STEP * ay
    nx = ext_ref[0] + HALF * (u + nu)
    ny = ext_ref[1] + HALF * (v + nv)
    nr = rho + TIME_STEP * ar
    low = jnp.where(occ > 0.0, nr, 1000000000.0)
    lows = []
    for c in range(NX):
        at = slice((c + HALO) * SLOTS + BASE, (c + HALO) * SLOTS + BASE + NY)
        for f, val in enumerate((nx, ny, nu, nv, nr)):
            new_ref[f, c] = jnp.where(occ[at] > 0.0, val[at], 0.0)
        lows.append(low[at])
    low_ref[...] = jnp.broadcast_to(jnp.min(jnp.concatenate(lows, axis=0)), low_ref.shape)


def scratch():
    return [
        pltpu.VMEM((SUMF * PLANE_ROWS, S), jnp.float32),
        pltpu.VMEM((NB, TALL, S), jnp.bfloat16),
        *[pltpu.VMEM((NB, S), jnp.float32) for _ in range(5)],
        pltpu.VMEM((NB * SUMF, S), jnp.float32),
        pltpu.VMEM((NB * EXTRA, S), jnp.float32),
    ]


def inner_kernel(mid_ref, inner_ref, tick_ref, *refs):
    tick_ref[...] = jnp.zeros_like(tick_ref)
    edge = jnp.zeros((BASE, S), jnp.float32)

    def grid(f):
        return jnp.concatenate([rows for c in range(NX) for rows in (edge, mid_ref[f, c], edge)], axis=0)

    rho = grid(4)
    occ = jnp.where(rho > 0.0, 1.0, 0.0)
    x = (grid(0) - 0.5) * occ
    y = (grid(1) - 0.5) * occ
    build(x, y, grid(2) * occ, grid(3) * occ, rho, occ, OWN, OWN, OWN + NX * SLOTS, refs)
    sweep_inner(refs)
    inner_ref[...] = refs[-2][OWN * SUMF : (OWN + NX * SLOTS) * SUMF, :]


def sph_inner(mid):
    return pl.pallas_call(
        inner_kernel,
        out_shape=(
            jax.ShapeDtypeStruct((NX * SLOTS * SUMF, S), jnp.float32),
            jax.ShapeDtypeStruct((8, S), jnp.float32),
        ),
        in_specs=[pl.BlockSpec(memory_space=pltpu.VMEM)],
        out_specs=(pl.BlockSpec(memory_space=pltpu.VMEM), pl.BlockSpec(memory_space=pltpu.VMEM)),
        scratch_shapes=scratch(),
        cost_estimate=pl.CostEstimate(flops=8000000000, transcendentals=0, bytes_accessed=1000000),
        name="sph_inner",
    )(mid)


def sph_step(*pieces):
    return pl.pallas_call(
        step_kernel,
        out_shape=(
            jax.ShapeDtypeStruct((5, NX, NY, S), jnp.float32),
            jax.ShapeDtypeStruct((PLANE, S), jnp.float32),
        ),
        in_specs=[pl.BlockSpec(memory_space=pltpu.VMEM)] * 6,
        out_specs=(
            pl.BlockSpec(memory_space=pltpu.VMEM),
            pl.BlockSpec(memory_space=pltpu.VMEM),
        ),
        scratch_shapes=[pltpu.VMEM((5, NB, S), jnp.float32), *scratch()],
        name="sph_step",
    )(*pieces)


def swap(x, dim, axis, wrap, tick=None):
    size, length = lax.axis_size(axis), x.shape[dim]
    even = lax.axis_index(axis) % 2 == 0
    last = lax.slice_in_dim(x, length - HALO, length, axis=dim)
    first = lax.slice_in_dim(x, 0, HALO, axis=dim)
    if tick is not None:
        last, first = last + tick, first + tick

    def pairs(start):
        ends = [(i, (i + 1) % size) for i in range(start, size if wrap else size - 1, 2)]
        return ends + [(j, i) for i, j in ends]

    far = lax.ppermute(jnp.where(even, first, last), axis, pairs(1))
    near = lax.ppermute(jnp.where(even, last, first), axis, pairs(0))
    return jnp.where(even, far, near), jnp.where(even, near, far)


def minimum_everywhere(low):
    chan, cross = lax.axis_size("chan"), lax.axis_size("cross")
    planes = {}
    for i in range(chan * cross):
        planes.setdefault((i // cross // 4 % 8, i % cross // 2), []).append(i)
    planes = list(planes.values())
    lines = [list(line) for line in zip(*planes)]
    both = ("chan", "cross")
    got = lax.all_to_all(low, both, 0, 0, tiled=True, axis_index_groups=planes)
    got = jnp.broadcast_to(jnp.min(got, axis=0, keepdims=True), (len(planes), S))
    return jnp.min(lax.all_to_all(got, both, 0, 0, tiled=True, axis_index_groups=lines))


def body(positions, velocity, density, counts):
    slot_index = jnp.arange(S, dtype=jnp.int32)
    rho = jnp.where(slot_index[None, None, :] < counts[:, :, None], density, 0.0)
    fields = jnp.concatenate([positions, velocity, rho[None]], axis=0)
    before, after = swap(fields, 1, "chan", True)
    wide = jnp.concatenate([before, fields, after], axis=1)
    inner, tick = sph_inner(fields)
    below, above = swap(wide, 2, "cross", False, tick[0, 0])
    new_fields, low = sph_step(fields, before, after, below, above, inner)
    return (new_fields, minimum_everywhere(low))


def solution(mesh):
    return jax.shard_map(
        body,
        mesh=mesh,
        in_specs=(
            P(None, "chan", "cross", None),
            P(None, "chan", "cross", None),
            P("chan", "cross", None),
            P("chan", "cross"),
        ),
        out_specs=(P(None, "chan", "cross", None), P()),
        check_vma=False,
    )
```

```python
import functools
import math

import jax
import jax.numpy as jnp
from jax import lax
from jax.experimental import pallas as pl
from jax.experimental.pallas import tpu as pltpu
from jax.sharding import PartitionSpec as P

SOUND_SQ = 100.0
KERNEL_GRAD = 140.0 / math.pi
PARTICLE_MASS = 1.0 / 128.0
GRAVITY = 1.0
TIME_STEP = 0.025
FORCE_SCALE = KERNEL_GRAD * PARTICLE_MASS
HALF = 0.5 * TIME_STEP

S = 128
NX = 4
NY = 16
HALO = 2
COLS = NX + 2 * HALO
SLOTS = NY + 2 * HALO + 4
BASE = HALO + 2
NB = COLS * SLOTS
PLANE_ROWS = NB + 8
SUMF = 24
EXTRA = 8
TALL = 32
OFFSETS = ((0, 0), (0, 1), (1, -1), (1, 0), (1, 1))
DIRECT = (0, 1)
CHAIN = 2
OWN = HALO * SLOTS
FAR = 1000.0
PLANE = 32


def split(x, pieces):
    out = []
    for _ in range(pieces - 1):
        h = x.astype(jnp.bfloat16).astype(jnp.float32)
        out.append(h)
        x = x - h
    out.append(x)
    return out


def on_grid(x, y, first=0):
    row = first + lax.broadcasted_iota(jnp.int32, x.shape, 0)
    col = (row * 171) >> 12
    slot = row - col * SLOTS
    return (
        x + (col.astype(jnp.float32) - 0.5 * (COLS - 1)),
        y + (slot.astype(jnp.float32) - 0.5 * (SLOTS - 1)),
    )


def build(x, y, u, v, rho, occ, first, low, high, refs):
    plane_ref, turned_ref, gx_ref, gy_ref, p_ref, u_ref, v_ref, acc_ref, extra_ref = refs
    acc_ref[...] = jnp.zeros_like(acc_ref)
    extra_ref[...] = jnp.zeros_like(extra_ref)
    gx, gy = on_grid(x, y, first)
    n = x.shape[0]
    at = slice(first, first + n)
    gx_ref[at] = jnp.where(occ > 0.0, gx, FAR)
    gy_ref[at] = gy
    p = SOUND_SQ * (rho - 1.0) * occ
    p_ref[at] = p
    u_ref[at] = u
    v_ref[at] = v
    gx = gx * occ
    gy = gy * occ
    rows = [occ] + split(gx, 3) + split(gy, 3) + split(u, 2) + split(v, 2) + split(u * gx + v * gy, 3)
    rows += split(p, 2) + split(p * gx, 3) + split(p * gy, 3)
    rows += [jnp.zeros((n, S), jnp.float32)] * (SUMF - len(rows))
    for f, val in enumerate(rows):
        plane_ref[f * PLANE_ROWS + first : f * PLANE_ROWS + first + n, :] = val

    def turn(r, carry):
        block = plane_ref[pl.ds(r, SUMF, stride=PLANE_ROWS), :]
        block = jnp.concatenate([block, jnp.zeros((TALL - SUMF, S), jnp.float32)], axis=0)
        turned_ref[r] = block.astype(jnp.bfloat16)
        return carry

    lax.fori_loop(low, high, turn, 0, unroll=8)


def geometry(a, bins, refs):
    gx_ref, gy_ref = refs[2], refs[3]
    ax = down(gx_ref, a)
    ay = down(gy_ref, a)
    for b in bins:
        dx = ax - gx_ref[pl.ds(b, 1), :]
        dy = ay - gy_ref[pl.ds(b, 1), :]
        t = dx * dx + dy * dy
        q = jnp.maximum(1.0 - t * lax.rsqrt(jnp.maximum(t, 1e-30)), 0.0)
        yield b, dx, dy, q * q * q


def down(ref, a):
    return jnp.broadcast_to(ref[pl.ds(a, 1), :], (S, S)).T


def column_sums(chain, ks, fine, refs):
    turned_ref = refs[1]
    direct = DIRECT if fine else ()
    p_ref, u_ref, v_ref, acc_ref, extra_ref = refs[4:9]
    out = []
    tiles = []
    for a in chain:
        bins = [a + OFFSETS[k][0] * SLOTS + OFFSETS[k][1] for k in ks]
        rows = []
        mine = {}
        for k, (b, dx, dy, w) in zip(ks, geometry(a, bins, refs)):
            if k not in direct:
                mine[k] = [w.astype(jnp.bfloat16)]
                if fine:
                    mine[k].append((w - mine[k][0].astype(jnp.float32)).astype(jnp.bfloat16))
                continue
            if not rows:
                ap, au, av = (down(ref, a) for ref in (p_ref, u_ref, v_ref))
            at = pl.ds(b, 1)
            wx = w * dx
            wy = w * dy
            p = ap + p_ref[at, :]
            vals = (p * wx, p * wy, (au - u_ref[at, :]) * wx + (av - v_ref[at, :]) * wy)
            rows = [r + x for r, x in zip(rows, vals)] if rows else list(vals)
            if k != 0:
                fx, fy, co = (jnp.sum(x, axis=0, keepdims=True) for x in vals)
                out.append((extra_ref, b * EXTRA, fill_rows(-fx, -fy, co)))
        if rows:
            rows = [jnp.sum(r.T, axis=0, keepdims=True) for r in rows]
            out.append((extra_ref, a * EXTRA, fill_rows(*rows)))
        tiles.append(mine)
        others = [k for k in mine if k != 0]
        to_b = sum(
            jnp.dot(turned_ref[a], jnp.concatenate([mine[k][n] for k in others], axis=1), preferred_element_type=jnp.float32)
            for n in range(2 if fine else 1)
        )
        for n, k in enumerate(others):
            b = a + OFFSETS[k][0] * SLOTS + OFFSETS[k][1]
            out.append((acc_ref, b * SUMF, to_b[:SUMF, n * S : (n + 1) * S]))
    base = chain[0]
    partners = sorted({(OFFSETS[k][0], OFFSETS[k][1] + m) for m, mine in enumerate(tiles) for k in mine})
    right = jnp.concatenate([turned_ref[base + i * SLOTS + j] for i, j in partners], axis=1)
    none = jnp.zeros((S, S), jnp.bfloat16)
    to_a = 0.0
    for n in range(2 if fine else 1):
        w = []
        for m, mine in enumerate(tiles):
            at = {(OFFSETS[k][0], OFFSETS[k][1] + m): mine[k][n] for k in mine}
            w.append(jnp.concatenate([at.get(ij, none) for ij in partners], axis=1))
        w = jnp.concatenate(w, axis=0)
        to_a = to_a + lax.dot_general(right, w, (((1,), (1,)), ((), ())), preferred_element_type=jnp.float32)
    for m, a in enumerate(chain):
        out.append((acc_ref, a * SUMF, to_a[:SUMF, m * S : (m + 1) * S]))
    return out


def fill_rows(*rows):
    return jnp.concatenate([*rows, jnp.zeros((8 - len(rows), S), jnp.float32)], axis=0)


def interact(many, ks, fine, refs):
    sums = [column_sums(chain, ks, fine, refs) for chain in many]
    for group in sums:
        for ref, row, val in group:
            at = pl.ds(pl.multiple_of(row, 8), val.shape[0])
            ref[at, :] = ref[at, :] + val


def chains(bins):
    return [[a + n for n in range(CHAIN)] for a in bins]


ALL = (0, 1, 2, 3, 4)
NEXT = (2, 3, 4)
SAME = (0, 1)
LOW = BASE + 1


def sweep_inner(start, stop, refs):
    def row(t, carry):
        s = LOW + CHAIN * t
        interact(chains([c * SLOTS + s for c in range(HALO, HALO + NX - 1)]), ALL, False, refs)
        interact(chains([(HALO + NX - 1) * SLOTS + s]), SAME, False, refs)
        return carry

    lax.fori_loop(start, stop, row, 0)


def sweep_outer(refs):
    last = HALO + NX

    def side(t, carry):
        s = LOW - CHAIN + 3 * CHAIN * t
        bins = [c * SLOTS + s + CHAIN * m for m in range(3) for c in (HALO - 1, last)]
        interact(chains(bins), ALL, False, refs)
        return carry

    lax.fori_loop(0, (NY + 2) // (3 * CHAIN), side, 0)

    def end(t, carry):
        s = LOW - CHAIN + t * (NY)
        interact(chains([c * SLOTS + s for c in range(HALO, last)]), ALL, False, refs)
        return carry

    lax.fori_loop(0, 2, end, 0)
    interact(chains([(last - 1) * SLOTS + LOW + CHAIN * m for m in range((NY - 2) // CHAIN)]), NEXT, False, refs)


def sweep_all(ring, fine, many, refs):
    c0, c1 = ring + 1, COLS - 2 - ring
    s0, s1 = ring + 3, SLOTS - 4 - ring
    wide, tall = c1 - c0 + 1, s1 - s0 + 1
    step = wide // many

    def column(c, carry):
        def row(t, carry):
            a = c * SLOTS + s0 + CHAIN * t
            interact(chains([a + step * m * SLOTS for m in range(many)]), ALL, fine, refs)
            return carry

        return lax.fori_loop(0, tall // CHAIN, row, carry)

    lax.fori_loop(c0, c0 + step, column, 0)


def sweep_rim(ring, fine, refs):
    c0, c1 = ring + 1, COLS - 2 - ring
    s0, s1 = ring + 3, SLOTS - 4 - ring
    wide, tall = c1 - c0 + 1, s1 - s0 + 1

    def bottom(t, carry):
        interact([[(c0 + 2 * t + m) * SLOTS + s0 - 1] for m in range(2)], (1, 4), fine, refs)
        return carry

    lax.fori_loop(0, wide // 2, bottom, 0)
    n = tall + 2
    total = n + wide - 1
    group = 5 if total % 5 == 0 else 7 if total % 7 == 0 else 1

    def rim(i, carry):
        ts = [i * group + m for m in range(group)]
        at = [jnp.where(t < n, (c0 - 1) * SLOTS + s0 - 1 + t, (c0 + t - n) * SLOTS + s1 + 1) for t in ts]
        interact([[a] for a in at], NEXT, fine, refs)
        return carry

    lax.fori_loop(0, total // group, rim, 0)


def gather_rates(x, y, u, v, rho, occ, fine, acc_ref, extra_ref):
    def get(f):
        return acc_ref[pl.ds(f, NB, stride=SUMF), :]

    gx, gy = on_grid(x, y)
    s1 = get(0)
    dx = gx * s1 - (get(1) + (get(2) + get(3)))
    dy = gy * s1 - (get(4) + (get(5) + get(6)))
    se = get(11) + (get(12) + get(13))
    comp = u * dx + v * dy - (gx * (get(7) + get(8)) + gy * (get(9) + get(10)) - se)
    p = SOUND_SQ * (rho - 1.0) * occ
    sp = get(14) + get(15)
    fx = p * dx + (gx * sp - (get(16) + (get(17) + get(18))))
    fy = p * dy + (gy * sp - (get(19) + (get(20) + get(21))))
    if fine:
        own = [extra_ref[pl.ds(f, NB, stride=EXTRA), :] for f in range(3)]
        fx = fx + own[0]
        fy = fy + own[1]
        comp = comp + own[2]
    return FORCE_SCALE * fx, FORCE_SCALE * fy - GRAVITY, -FORCE_SCALE * comp


def step_kernel(mid_ref, before_ref, after_ref, below_ref, above_ref, inner_ref, more_ref, new_ref, low_ref, ext_ref, *refs):
    acc_ref = refs[-2]
    edge = jnp.zeros((BASE - HALO, S), jnp.float32)
    for f in range(5):
        for c in range(COLS):
            if c < HALO:
                mid = before_ref[f, c]
            elif c < HALO + NX:
                mid = mid_ref[f, c - HALO]
            else:
                mid = after_ref[f, c - HALO - NX]
            rows = [edge, below_ref[f, c], mid, above_ref[f, c], edge]
            ext_ref[f, c * SLOTS : (c + 1) * SLOTS, :] = jnp.concatenate(rows, axis=0)

    def load():
        rho = ext_ref[4]
        occ = jnp.where(rho > 0.0, 1.0, 0.0)
        x = (ext_ref[0] - 0.5) * occ
        y = (ext_ref[1] - 0.5) * occ
        return x, y, ext_ref[2] * occ, ext_ref[3] * occ, rho, occ

    x, y, u, v, rho, occ = load()
    build(x, y, u, v, rho, occ, 0, 0, NB, refs)
    acc_ref[OWN * SUMF : (OWN + NX * SLOTS) * SUMF, :] = inner_ref[...] + more_ref[...]
    sweep_outer(refs)
    sweep_rim(0, False, refs)
    x, y, u, v, rho, occ = load()
    ax, ay, ar = gather_rates(x, y, u, v, rho, occ, False, *refs[-2:])

    def predicted():
        return (
            (x + HALF * u) * occ,
            (y + HALF * v) * occ,
            (u + HALF * ax) * occ,
            (v + HALF * ay) * occ,
            (rho + HALF * ar) * occ,
        )

    px, py, pu, pv, pr = predicted()
    build(px, py, pu, pv, pr, occ, 0, SLOTS, NB - SLOTS, refs)
    sweep_all(1, True, 4, refs)
    sweep_rim(1, True, refs)
    ax, ay, ar = gather_rates(px, py, pu, pv, pr, occ, True, *refs[-2:])
    x, y, u, v, rho, occ = load()
    nu = u + TIME_STEP * ax
    nv = v + TIME_STEP * ay
    nx = ext_ref[0] + HALF * (u + nu)
    ny = ext_ref[1] + HALF * (v + nv)
    nr = rho + TIME_STEP * ar
    low = jnp.where(occ > 0.0, nr, 1000000000.0)
    lows = []
    for c in range(NX):
        at = slice((c + HALO) * SLOTS + BASE, (c + HALO) * SLOTS + BASE + NY)
        for f, val in enumerate((nx, ny, nu, nv, nr)):
            new_ref[f, c] = jnp.where(occ[at] > 0.0, val[at], 0.0)
        lows.append(low[at])
    low_ref[...] = jnp.broadcast_to(jnp.min(jnp.concatenate(lows, axis=0)), low_ref.shape)


def scratch():
    return [
        pltpu.VMEM((SUMF * PLANE_ROWS, S), jnp.float32),
        pltpu.VMEM((NB, TALL, S), jnp.bfloat16),
        *[pltpu.VMEM((NB, S), jnp.float32) for _ in range(5)],
        pltpu.VMEM((NB * SUMF, S), jnp.float32),
        pltpu.VMEM((NB * EXTRA, S), jnp.float32),
    ]


def inner_kernel(start, stop, mid_ref, inner_ref, tick_ref, *refs):
    tick_ref[...] = jnp.zeros_like(tick_ref)
    edge = jnp.zeros((BASE, S), jnp.float32)

    def grid(f):
        return jnp.concatenate([rows for c in range(NX) for rows in (edge, mid_ref[f, c], edge)], axis=0)

    rho = grid(4)
    occ = jnp.where(rho > 0.0, 1.0, 0.0)
    x = (grid(0) - 0.5) * occ
    y = (grid(1) - 0.5) * occ
    build(x, y, grid(2) * occ, grid(3) * occ, rho, occ, OWN, OWN, OWN + NX * SLOTS, refs)
    sweep_inner(start, stop, refs)
    inner_ref[...] = refs[-2][OWN * SUMF : (OWN + NX * SLOTS) * SUMF, :]


def sph_inner(mid, start, stop):
    return pl.pallas_call(
        functools.partial(inner_kernel, start, stop),
        out_shape=(
            jax.ShapeDtypeStruct((NX * SLOTS * SUMF, S), jnp.float32),
            jax.ShapeDtypeStruct((1, S), jnp.float32),
        ),
        in_specs=[pl.BlockSpec(memory_space=pltpu.VMEM)],
        out_specs=(pl.BlockSpec(memory_space=pltpu.VMEM), pl.BlockSpec(memory_space=pltpu.VMEM)),
        scratch_shapes=scratch(),
        cost_estimate=pl.CostEstimate(flops=4000000000, transcendentals=0, bytes_accessed=1000000),
    )(mid)


def sph_step(*pieces):
    return pl.pallas_call(
        step_kernel,
        out_shape=(
            jax.ShapeDtypeStruct((5, NX, NY, S), jnp.float32),
            jax.ShapeDtypeStruct((PLANE, S), jnp.float32),
        ),
        in_specs=[pl.BlockSpec(memory_space=pltpu.VMEM)] * 7,
        out_specs=(
            pl.BlockSpec(memory_space=pltpu.VMEM),
            pl.BlockSpec(memory_space=pltpu.VMEM),
        ),
        scratch_shapes=[pltpu.VMEM((5, NB, S), jnp.float32), *scratch()],
        name="sph_step",
    )(*pieces)


def swap(x, dim, axis, wrap, tick=None):
    size, length = lax.axis_size(axis), x.shape[dim]
    even = lax.axis_index(axis) % 2 == 0
    last = lax.slice_in_dim(x, length - HALO, length, axis=dim)
    first = lax.slice_in_dim(x, 0, HALO, axis=dim)
    if tick is not None:
        last, first = last + tick, first + tick

    def pairs(start):
        ends = [(i, (i + 1) % size) for i in range(start, size if wrap else size - 1, 2)]
        return ends + [(j, i) for i, j in ends]

    far = lax.ppermute(jnp.where(even, first, last), axis, pairs(1))
    near = lax.ppermute(jnp.where(even, last, first), axis, pairs(0))
    return jnp.where(even, far, near), jnp.where(even, near, far)


def minimum_everywhere(low):
    chan, cross = lax.axis_size("chan"), lax.axis_size("cross")
    planes = {}
    for i in range(chan * cross):
        planes.setdefault((i // cross // 4 % 8, i % cross // 2), []).append(i)
    planes = list(planes.values())
    lines = [list(line) for line in zip(*planes)]
    both = ("chan", "cross")
    got = lax.all_to_all(low, both, 0, 0, tiled=True, axis_index_groups=planes)
    got = jnp.broadcast_to(jnp.min(got, axis=0, keepdims=True), (len(planes), S))
    return jnp.min(lax.all_to_all(got, both, 0, 0, tiled=True, axis_index_groups=lines))


def body(positions, velocity, density, counts):
    slot_index = jnp.arange(S, dtype=jnp.int32)
    rho = jnp.where(slot_index[None, None, :] < counts[:, :, None], density, 0.0)
    fields = jnp.concatenate([positions, velocity, rho[None]], axis=0)
    before, after = swap(fields, 1, "chan", True)
    wide = jnp.concatenate([before, fields, after], axis=1)
    half = (NY - 2) // CHAIN // 2
    inner, tick = sph_inner(fields, 0, half)
    more, _ = sph_inner(fields, half, (NY - 2) // CHAIN)
    below, above = swap(wide, 2, "cross", False, tick.reshape(S))
    new_fields, low = sph_step(fields, before, after, below, above, inner, more)
    return (new_fields, minimum_everywhere(low))


def solution(mesh):
    return jax.shard_map(
        body,
        mesh=mesh,
        in_specs=(
            P(None, "chan", "cross", None),
            P(None, "chan", "cross", None),
            P("chan", "cross", None),
            P("chan", "cross"),
        ),
        out_specs=(P(None, "chan", "cross", None), P()),
        check_vma=False,
    )
```
